256 devices in a mesh: ty: 16 (over y_hi, x, core), tx: 16 (over z, y_lo).
Axes of the slice: x: 4, y: 4 (y_hi: 2, y_lo: 2; y = y_hi * 2 + y_lo), z: 8, core: 2. Of those that a mesh axis runs over, the one named last changes fastest.
Arguments:
- object_field: float32 [2, 4096, 4096], P(None, 'ty', 'tx'), may hold values from -6 to 6
- probe_modes: float32 [2, 2, 256, 256], replicated, may hold values from -6 to 6
- intensities: float32 [16, 16, 3, 256, 256], P('ty', 'tx'), may hold values from 0.25 to 16
- offsets: int32 [16, 16, 3, 2], P('ty', 'tx'), may hold values from 0 to 256
- counts: int32 [16, 16], replicated, may hold values from 1 to 3, as said below
Outputs:
- object_grad: float32 [2, 4096, 4096], P(None, 'ty', 'tx')
- probe_grad: float32 [2, 2, 256, 256], replicated
The draws below stay inside these ranges and needn't reach their ends.
Inputs may be any that keep to these rules, and one draw needn't show every extreme that they name: Tile (a, b) uses slots 0 to counts[a, b] - 1 of intensities and offsets; its other slots are ignored. In every draw some tile uses all 3 slots.
All inputs are finite; a program needn't handle non-finite values.
Results may differ from the reference program's by a relative error of at most 0.0003.
Values sent between devices are 32-bit elements; how exact they have to be, the bound alone decides.
A program may use at most 64 MiB of HBM per device.

```python
import jax
import jax.numpy as jnp
from jax import lax

P_SIZE = 256
MODES = 2
TILE = 256
CAP = 3
NY = 4096
NX = 4096
N_TY = 16
N_TX = 16


def draw_counts(key, part):
    first_key, second_key = jax.random.split(key)
    levels = jax.random.randint(first_key, (N_TY * N_TX,), 0, 65)
    listed = 1 + (CAP - 1) * levels * levels // 4096
    chosen = jax.random.randint(second_key, (), 0, N_TY * N_TX)
    listed = jnp.where(jnp.arange(N_TY * N_TX, dtype=jnp.int32) == chosen, CAP, listed)
    return listed.reshape(N_TY, N_TX).astype(jnp.int32)


def place_ends(result, own_key, smallest, top_value):
    place = [jax.random.randint(jax.random.fold_in(own_key, axis), (), 0, length) for axis, length in enumerate(result.shape)]
    widest = result.shape.index(max(result.shape))
    neighbour = place[:widest] + [(place[widest] + 1) % result.shape[widest]] + place[widest + 1:]
    return result.at[tuple(place)].set(smallest).at[tuple(neighbour)].set(top_value)


def steps_of(stream_key, extent, cuts, low, high):
    loudness = 1.0
    for position, shards_of in cuts:
        heights = jax.random.uniform(jax.random.fold_in(jax.random.fold_in(stream_key, 6), position), (shards_of,), jnp.float32, low / len(cuts), high / len(cuts))
        loudness = loudness * jnp.repeat(jnp.exp(heights), extent[position] // shards_of).reshape((-1,) + (1,) * (len(extent) - 1 - position))
    return loudness


def gaussian(stream_key, extent, scale, bound, cuts=(), kind=jnp.bfloat16):
    values = jax.random.normal(stream_key, extent, jnp.float32) * scale
    if len(cuts) > 0:
        values = steps_of(stream_key, extent, cuts, -0.22, 0.18) * values
    return jnp.clip(values, min=-bound, max=bound).astype(kind)


def setup_inputs(seed: int = 0) -> dict:
    key_of = jax.random.split(jax.random.key(seed), 6)
    return {
        "object_field": gaussian(key_of[0], (2, NY, NX), 1.0, 6.0, ((1, 16), (2, 16)), jnp.float32),
        "probe_modes": gaussian(key_of[1], (2, MODES, P_SIZE, P_SIZE), 0.7, 6.0, (), jnp.float32),
        "intensities": jnp.clip(0.25 + 15.75 * jax.random.uniform(key_of[2], (N_TY, N_TX, CAP, P_SIZE, P_SIZE), jnp.float32) ** steps_of(key_of[2], (N_TY, N_TX, CAP, P_SIZE, P_SIZE), ((0, 16), (1, 16)), -0.2, 0.2), 0.25, 16.0),
        "offsets": place_ends(jax.random.randint(key_of[3], (N_TY, N_TX, CAP, 2), 0, TILE + 1), jax.random.fold_in(key_of[3], 1), 0, TILE).astype(jnp.int32),
        "counts": draw_counts(jax.random.fold_in(key_of[5], 71), 0),
    }


FLOOR = 0.5

def reference(object_field, probe_modes, intensities, offsets, counts):
    margin = P_SIZE // 2
    padded = jnp.pad(object_field, ((0, 0), (margin, margin), (margin, margin)))
    complex_object = padded[0] + 1j * padded[1]
    probe = probe_modes[0] + 1j * probe_modes[1]
    total_slots = N_TY * N_TX * CAP

    def visit(carry, slot_index):
        grid, probe_sum = carry
        tile_row = (slot_index // (N_TX * CAP)).astype(jnp.int32)
        tile_col = (slot_index // CAP % N_TX).astype(jnp.int32)
        within = (slot_index % CAP).astype(jnp.int32)
        weight = (within < counts[tile_row, tile_col]).astype(jnp.float32)
        row_start = (tile_row * TILE + offsets[tile_row, tile_col, within, 0]).astype(jnp.int32)
        col_start = (tile_col * TILE + offsets[tile_row, tile_col, within, 1]).astype(jnp.int32)
        patch = lax.dynamic_slice(complex_object, (row_start, col_start), (P_SIZE, P_SIZE))
        far_field = jnp.fft.fft2(probe * patch, norm='ortho')
        amplitude = jnp.sqrt(lax.optimization_barrier(jnp.sum(jnp.real(far_field) * jnp.real(far_field) + jnp.imag(far_field) * jnp.imag(far_field), axis=0)))
        factor = 1.0 - jnp.sqrt(intensities[tile_row, tile_col, within]) / jnp.maximum(amplitude, FLOOR)
        backward = jnp.fft.ifft2(far_field * factor, norm='ortho')
        object_part = lax.optimization_barrier(jnp.sum(jnp.conj(probe) * backward, axis=0)) * weight
        current = lax.dynamic_slice(grid, (row_start, col_start), (P_SIZE, P_SIZE))
        grid = lax.dynamic_update_slice(grid, current + object_part, (row_start, col_start))
        probe_sum = probe_sum + jnp.conj(patch) * backward * weight
        return ((grid, probe_sum), None)
    start_carry = (jnp.zeros_like(complex_object), jnp.zeros_like(probe))
    (grid, probe_sum), _ = lax.scan(visit, start_carry, jnp.arange(total_slots, dtype=jnp.int32))
    inner = grid[margin:-margin, margin:-margin]
    object_grad = jnp.stack([jnp.real(inner), jnp.imag(inner)]).astype(jnp.float32)
    probe_total = probe_sum / (N_TY * N_TX)
    probe_grad = jnp.stack([jnp.real(probe_total), jnp.imag(probe_total)]).astype(jnp.float32)
    return (object_grad, probe_grad)
```

```python
import functools

import jax
import jax.numpy as jnp
import numpy as np
from jax import lax
from jax.experimental import pallas as pl
from jax.experimental.pallas import tpu as pltpu
from jax.sharding import PartitionSpec as P

FLOOR = 0.5
MESH = pl.DeviceIdType.MESH
F32 = jnp.float32
BF16 = jnp.bfloat16
VMEM = pl.BlockSpec(memory_space=pltpu.VMEM)
SMEM = pl.BlockSpec(memory_space=pltpu.SMEM)


def tables(pattern):
    half = pattern // 2
    n = np.arange(half)[:, None]
    out = []
    for parity in (0, 1):
        k = 2 * np.arange(half)[None, :] + parity
        angle = 2.0 * np.pi * ((n * k) % pattern) / pattern
        c, s = np.cos(angle) / np.sqrt(pattern), np.sin(angle) / np.sqrt(pattern)
        full = np.block([[c, -s], [s, c]])
        hi = full.astype(BF16)
        lo = (full - hi.astype(np.float64)).astype(BF16)
        out.append((hi, lo))
    (eh, el), (oh, ol) = out
    right = np.stack([np.concatenate([h, h, l], 0) for h, l in out])
    right_back = np.stack([np.concatenate([h.T, h.T, l.T], 0) for h, l in out])
    left = np.stack([np.concatenate([h.T, h.T, l.T], 1) for h, l in out])
    left_back = np.stack([np.concatenate([h, h, l], 1) for h, l in out])
    return right, left, left_back, right_back


def reorder_table(pattern):
    half = pattern // 2
    table = np.zeros((pattern, pattern), np.float32)
    table[2 * np.arange(half), np.arange(half)] = 1
    table[2 * np.arange(half) + 1, half + np.arange(half)] = 1
    return table.astype(BF16)


def split(a):
    hi = a.astype(BF16)
    return hi, (a - hi.astype(F32)).astype(BF16)


def times_right(a, table):
    hi, lo = split(a)
    return jnp.dot(jnp.concatenate([hi, lo, hi], axis=1), table, preferred_element_type=F32)


def times_left(table, a):
    hi, lo = split(a)
    return jnp.dot(table, jnp.concatenate([hi, lo, hi], axis=0), preferred_element_type=F32)


def slots_kernel(
    counts, spots, ext, probe, measured, right, left, left_back, right_back, order, order_t,
    grid, probe_sum, factor,
):
    pattern = probe.shape[2]
    half = pattern // 2
    modes = probe.shape[1]
    wide, tall = pattern + half, pattern + 8
    listed = counts[lax.axis_index("ty"), lax.axis_index("tx")]
    grid[...] = jnp.zeros(grid.shape, F32)
    probe_sum[...] = jnp.zeros(probe_sum.shape, F32)

    @pl.loop(0, listed)
    def _(slot):
        row = spots[slot, 0]
        col = spots[slot, 1]
        block = (col >= half).astype(jnp.int32)
        rest = col - block * half
        first = pl.multiple_of(block * half, half)
        group = jnp.minimum(lax.div(row, 8), pattern // 8 - 1)
        skip = row - group * 8
        top_row = pl.multiple_of(group * 8, 8)

        def window(part):
            strip = ext[part, pl.ds(top_row, tall), pl.ds(first, wide)]
            strip = pltpu.roll(strip, lax.rem(tall - skip, tall), 0)[:pattern]
            return pltpu.roll(strip, lax.rem(wide - rest, wide), 1)[:, :pattern]

        xr, xi = window(0), window(1)

        root = jnp.sqrt(measured[slot])
        hi, lo = split(root)
        root = jnp.dot(hi, order[...], preferred_element_type=F32) + jnp.dot(
            lo, order[...], preferred_element_type=F32
        )
        hi, lo = split(root)
        root = jnp.dot(order_t[...], hi, preferred_element_type=F32) + jnp.dot(
            order_t[...], lo, preferred_element_type=F32
        )

        far = []
        for m in range(modes):
            pr, pi = probe[0, m], probe[1, m]
            wr = pr * xr - pi * xi
            wi = pr * xi + pi * xr
            u = jnp.concatenate([wr[:, :half] + wr[:, half:], wi[:, :half] + wi[:, half:]], 1)
            v = jnp.concatenate([wr[:, :half] - wr[:, half:], wi[:, :half] - wi[:, half:]], 1)
            even = times_right(u, right[0])
            odd = times_right(v, right[1])
            us = jnp.concatenate([even[:half] + even[half:], odd[:half] + odd[half:]], 1)
            vs = jnp.concatenate([even[:half] - even[half:], odd[:half] - odd[half:]], 1)
            us, vs = regroup(us, half), regroup(vs, half)
            far.append((times_left(left[0], us), times_left(left[1], vs)))

        for parity in (0, 1):
            power = 0.0
            for m in range(modes):
                g = far[m][parity]
                power = power + g[:half] * g[:half] + g[half:] * g[half:]
            amplitude = jnp.maximum(jnp.sqrt(power), FLOOR)
            factor[parity] = 1.0 - root[parity * half : (parity + 1) * half] / amplitude

        object_r = 0.0
        object_i = 0.0
        for m in range(modes):
            pr, pi = probe[0, m], probe[1, m]
            halves = []
            for parity in (0, 1):
                f = factor[parity]
                g = far[m][parity]
                halves.append(times_left(left_back[parity], jnp.concatenate([g[:half] * f, g[half:] * f], 0)))
            top, bottom = halves[0] + halves[1], halves[0] - halves[1]
            k = []
            for parity in (0, 1):
                at = slice(parity * half, (parity + 1) * half)
                z = jnp.concatenate(
                    [
                        jnp.concatenate([top[:half, at], top[half:, at]], 1),
                        jnp.concatenate([bottom[:half, at], bottom[half:, at]], 1),
                    ],
                    0,
                )
                k.append(times_right(z, right_back[parity]))
            near, off = k[0] + k[1], k[0] - k[1]
            br = jnp.concatenate([near[:, :half], off[:, :half]], 1)
            bi = jnp.concatenate([near[:, half:], off[:, half:]], 1)
            object_r = object_r + pr * br + pi * bi
            object_i = object_i + pr * bi - pi * br
            probe_sum[0, m] += xr * br + xi * bi
            probe_sum[1, m] += xr * bi - xi * br

        for part, piece in ((0, object_r), (1, object_i)):
            padded = jnp.concatenate([piece, jnp.zeros((pattern, half), F32)], 1)
            padded = pltpu.roll(padded, rest, 1)
            padded = jnp.concatenate([padded, jnp.zeros((8, wide), F32)], 0)
            grid[part, pl.ds(top_row, tall), pl.ds(first, wide)] += pltpu.roll(padded, skip, 0)


def regroup(a, half):
    re = jnp.concatenate([a[:, :half], a[:, 2 * half : 3 * half]], 1)
    im = jnp.concatenate([a[:, half : 2 * half], a[:, 3 * half :]], 1)
    return jnp.concatenate([re, im], 0)


def slots(counts, spots, ext, probe, measured):
    pattern = probe.shape[2]
    right, left, left_back, right_back = tables(pattern)
    order = reorder_table(pattern)
    extent = ext.shape[1]
    return pl.pallas_call(
        slots_kernel,
        out_shape=(
            jax.ShapeDtypeStruct(ext.shape, F32),
            jax.ShapeDtypeStruct(probe.shape, F32),
        ),
        in_specs=[SMEM, SMEM] + [VMEM] * 9,
        out_specs=(VMEM, VMEM),
        scratch_shapes=[pltpu.VMEM((2, pattern // 2, pattern), F32)],
        name="slots",
    )(
        counts, spots, ext, probe, measured,
        jnp.asarray(right), jnp.asarray(left), jnp.asarray(left_back), jnp.asarray(right_back),
        jnp.asarray(order), jnp.asarray(order.T),
    )


def remote(src, dst, send, recv, ty, tx):
    return pltpu.make_async_remote_copy(
        src_ref=src, dst_ref=dst, send_sem=send, recv_sem=recv, device_id=(ty, tx), device_id_type=MESH
    )


def neighbours():
    ty, tx = lax.axis_index("ty"), lax.axis_index("tx")
    n, m = lax.axis_size("ty"), lax.axis_size("tx")
    up, down = lax.rem(ty + n - 1, n), lax.rem(ty + 1, n)
    west, east = lax.rem(tx + m - 1, m), lax.rem(tx + 1, m)
    return ty, tx, n, m, up, down, west, east


def greet(peers):
    barrier = pltpu.get_barrier_semaphore()
    for ty, tx in peers:
        pl.semaphore_signal(barrier, inc=1, device_id=(ty, tx), device_id_type=MESH)
    pl.semaphore_wait(barrier, len(peers))


def halo_kernel(tile, ext, local, side_send, side_recv, rows_send, rows_recv):
    ty, tx, n, m, up, down, west, east = neighbours()
    cells = tile.shape[1]
    margin = cells // 2
    size = 2 * cells
    far = cells + margin
    greet([(up, tx), (down, tx), (ty, west), (ty, east)])

    core = lax.rem(ty, 2)
    copies = {}
    for step in range(2):
        h = core if step == 0 else 1 - core
        at = pl.multiple_of(h * margin, margin)
        src_rows = pl.ds(at, margin)
        dst_rows = pl.ds(pl.multiple_of(at + margin, margin), margin)
        for side, (peer, src, dst) in enumerate(
            ((east, pl.ds(margin, margin), pl.ds(0, margin)), (west, pl.ds(0, margin), pl.ds(far, margin)))
        ):
            copy = remote(
                tile.at[:, src_rows, src],
                ext.at[:, dst_rows, dst],
                side_send.at[step, side],
                side_recv.at[step, side],
                ty,
                peer,
            )
            copy.start()
            copies[step, side] = copy
    middle = pl.ds(margin, cells)
    to_up = remote(
        tile.at[:, pl.ds(0, margin), :], ext.at[:, pl.ds(far, margin), middle],
        rows_send.at[0, 0], rows_recv.at[0, 0], up, tx,
    )
    to_down = remote(
        tile.at[:, pl.ds(margin, margin), :], ext.at[:, pl.ds(0, margin), middle],
        rows_send.at[1, 0], rows_recv.at[1, 0], down, tx,
    )
    to_up.start()
    to_down.start()
    own = pltpu.make_async_copy(tile, ext.at[:, middle, middle], local)
    own.start()

    sides = (pl.ds(0, margin), pl.ds(far, margin))

    def corner(direction, side):
        if direction == 0:
            src, dst, peer = margin, far, up
        else:
            src, dst, peer = cells, 0, down
        return remote(
            ext.at[:, pl.ds(src, margin), sides[side]],
            ext.at[:, pl.ds(dst, margin), sides[side]],
            rows_send.at[direction, 1 + side],
            rows_recv.at[direction, 1 + side],
            peer,
            tx,
        )

    for step in range(2):
        for side in range(2):
            copies[step, side].wait_recv()
            for direction in range(2):

                @pl.when(core == (direction if step == 0 else 1 - direction))
                def _(direction=direction, side=side):
                    corner(direction, side).start()

    for step in range(2):
        for side in range(2):
            copies[step, side].wait_send()
    own.wait()
    to_up.wait()
    to_down.wait()
    for direction in range(2):
        for side in range(2):
            corner(direction, side).wait()

    for there, rows, cols in (
        (ty == 0, pl.ds(0, margin), pl.ds(0, size)),
        (ty == n - 1, pl.ds(far, margin), pl.ds(0, size)),
        (tx == 0, pl.ds(0, size), pl.ds(0, margin)),
        (tx == m - 1, pl.ds(0, size), pl.ds(far, margin)),
    ):

        @pl.when(there)
        def _(rows=rows, cols=cols):
            ext[:, rows, cols] = jnp.zeros((2, rows.size, cols.size), F32)


def halo(tile):
    cells = tile.shape[1]
    dma = pltpu.SemaphoreType.DMA
    return pl.pallas_call(
        halo_kernel,
        out_shape=jax.ShapeDtypeStruct((2, 2 * cells, 2 * cells), F32),
        in_specs=[VMEM],
        out_specs=VMEM,
        scratch_shapes=[dma(()), dma((2, 2)), dma((2, 2)), dma((2, 3)), dma((2, 3))],
        compiler_params=pltpu.CompilerParams(collective_id=0, has_side_effects=True),
        name="halo",
    )(tile)


def return_kernel(
    grid, part, inner, total,
    from_below, from_above, side_out, from_side, core_in, plane_in, line_in,
    rows_send, rows_recv, side_send, side_recv,
    core_send, core_recv, plane_send, plane_recv, line_send, line_recv,
    back_send, back_recv, pair_send, pair_recv,
):
    ty, tx, n, m, up, down, west, east = neighbours()
    cells = inner.shape[1]
    margin = cells // 2
    far = cells + margin
    core = lax.rem(ty, 2)
    mate = ty + 1 - 2 * core
    chip, lane, line = ty // 2, lax.rem(tx, 2), tx // 2
    plane_size, line_size = n, m // 2
    me = chip * 2 + lane

    def plane_peer(d):
        other = lax.rem(me + d, plane_size)
        return other, (other // 2) * 2 + core, line * 2 + lax.rem(other, 2)

    def line_peer(d):
        return lax.rem(line + d, line_size) * 2 + lane

    peers = [(up, tx), (down, tx), (ty, west), (ty, east)]
    peers.append((mate, tx))
    for d in range(1, plane_size):
        _, py, px = plane_peer(d)
        peers.append((py, px))
    for d in range(1, line_size):
        peers.append((ty, line_peer(d)))
    greet(peers)

    rows = part.shape[0]
    half = rows // 2
    piece = half // plane_size
    mine = pl.multiple_of(core * half, half)
    others = pl.multiple_of((1 - core) * half, half)

    swap = remote(part.at[pl.ds(others, half)], core_in, core_send, core_recv, mate, tx)
    swap.start()

    row_copies = {}
    cols = (pl.ds(0, margin), pl.ds(far, margin), pl.ds(margin, cells))
    for i, at in enumerate(cols):
        for direction, (src, dst, peer) in enumerate(
            ((pl.ds(0, margin), from_below, up), (pl.ds(far, margin), from_above, down))
        ):
            copy = remote(
                grid.at[:, src, at], dst.at[:, :, at], rows_send.at[direction, i], rows_recv.at[direction, i], peer, tx
            )
            copy.start()
            row_copies[direction, i] = copy

    swap.wait()
    core_in[...] = core_in[...] + part[pl.ds(mine, half), :]
    plane_copies = []
    for d in range(1, plane_size):
        other, py, px = plane_peer(d)
        copy = remote(
            core_in.at[pl.ds(pl.multiple_of(other * piece, piece), piece)],
            plane_in.at[d],
            plane_send.at[d],
            plane_recv.at[d],
            py,
            px,
        )
        copy.start()
        plane_copies.append(copy)

    side_copies = []
    for step in range(2):
        for source in range(2):
            lower = source == 0

            @pl.when(core == (source if step == 0 else 1 - source))
            def _(source=source, lower=lower):
                received = from_below if lower else from_above
                edge = ty == (n - 1 if lower else 0)
                src_row = cells if lower else margin
                for side in range(2):
                    row_copies[0 if lower else 1, side].wait_recv()
                    at = cols[side]
                    add = jnp.where(edge, 0.0, received[:, :, at])
                    side_out[side, 1 if lower else 0] = grid[:, pl.ds(src_row, margin), at] + add

        h = 1 - core if step == 0 else core
        for side, peer in ((0, west), (1, east)):
            copy = remote(
                side_out.at[side, h], from_side.at[side, h], side_send.at[side, step], side_recv.at[side, step], ty, peer
            )
            copy.start()
            side_copies.append(copy)

    for copy in plane_copies:
        copy.wait()
    own = core_in[pl.ds(pl.multiple_of(me * piece, piece), piece), :]
    for d in range(1, plane_size):
        own = own + plane_in[d]
    line_in[line] = own
    line_copies = []
    for d in range(1, line_size):
        copy = remote(
            line_in.at[line], line_in.at[line], line_send.at[d], line_recv.at[d], ty, line_peer(d)
        )
        copy.start()
        line_copies.append(copy)
    for copy in line_copies:
        copy.wait()
    done = line_in[0]
    for d in range(1, line_size):
        done = done + line_in[d]

    place = pl.ds(pl.multiple_of(mine + me * piece, piece), piece)
    total[place, :] = done
    back = []
    for d in range(1, plane_size):
        _, py, px = plane_peer(d)
        copy = remote(total.at[place], total.at[place], back_send.at[d], back_recv.at[d], py, px)
        copy.start()
        back.append(copy)
    pair = [remote(total.at[place], total.at[place], pair_send.at[0], pair_recv.at[0], mate, tx)]
    pair[0].start()
    for d in range(1, plane_size):
        back[d - 1].wait_recv()
        source = lax.rem(me + plane_size - d, plane_size)
        at = pl.ds(pl.multiple_of(mine + source * piece, piece), piece)
        copy = remote(total.at[at], total.at[at], pair_send.at[d], pair_recv.at[d], mate, tx)
        copy.start()
        pair.append(copy)

    for direction in range(2):
        row_copies[direction, 2].wait_recv()
    for copy in side_copies:
        copy.wait()
    middle = pl.ds(margin, cells)
    for h in range(2):
        received = from_above if h == 0 else from_below
        edge = ty == (0 if h == 0 else n - 1)
        value = grid[:, pl.ds(margin + h * margin, margin), middle] + jnp.where(edge, 0.0, received[:, :, middle])
        from_west = jnp.where(tx == 0, 0.0, from_side[1, h])
        from_east = jnp.where(tx == m - 1, 0.0, from_side[0, h])
        inner[:, pl.ds(h * margin, margin), :] = value + jnp.concatenate([from_west, from_east], 2)

    for key in row_copies:
        row_copies[key].wait_send()
    for copy in back:
        copy.wait_send()
    for copy in pair:
        copy.wait()


def give_back(grid, part):
    cells = grid.shape[1] // 2
    margin = cells // 2
    rows, width = part.shape
    n, m = lax.axis_size("ty"), lax.axis_size("tx")
    plane, line = n, m // 2
    piece = rows // 2 // plane
    dma = pltpu.SemaphoreType.DMA
    return pl.pallas_call(
        return_kernel,
        out_shape=(
            jax.ShapeDtypeStruct((2, cells, cells), F32),
            jax.ShapeDtypeStruct(part.shape, F32),
        ),
        in_specs=[VMEM, VMEM],
        out_specs=(VMEM, VMEM),
        scratch_shapes=[
            pltpu.VMEM((2, margin, 2 * cells), F32),
            pltpu.VMEM((2, margin, 2 * cells), F32),
            pltpu.VMEM((2, 2, 2, margin, margin), F32),
            pltpu.VMEM((2, 2, 2, margin, margin), F32),
            pltpu.VMEM((rows // 2, width), F32),
            pltpu.VMEM((plane, piece, width), F32),
            pltpu.VMEM((line, piece, width), F32),
            dma((2, 3)), dma((2, 3)), dma((2, 2)), dma((2, 2)),
            dma(()), dma(()), dma((plane,)), dma((plane,)), dma((line,)), dma((line,)),
            dma((plane,)), dma((plane,)), dma((plane,)), dma((plane,)),
        ],
        compiler_params=pltpu.CompilerParams(collective_id=1, has_side_effects=True),
        name="give_back",
    )(grid, part)


def shards(object_field, probe_modes, intensities, offsets, counts):
    ext = halo(object_field)
    grid, part = slots(counts, offsets[0, 0], ext, probe_modes, intensities[0, 0])
    inner, total = give_back(grid, part.reshape(-1, part.shape[-1]))
    count = lax.axis_size("ty") * lax.axis_size("tx")
    return inner, total.reshape(probe_modes.shape) * (1.0 / count)


def solution(mesh):
    placed = (
        P(None, "ty", "tx"),
        P(),
        P("ty", "tx", None, None, None),
        P("ty", "tx", None, None),
        P(),
    )
    return jax.shard_map(
        shards, mesh=mesh, in_specs=placed, out_specs=(P(None, "ty", "tx"), P()), check_vma=False
    )
```

```python
import functools

import jax
import jax.numpy as jnp
import numpy as np
from jax import lax
from jax.experimental import pallas as pl
from jax.experimental.pallas import tpu as pltpu
from jax.sharding import PartitionSpec as P

FLOOR = 0.5
MESH = pl.DeviceIdType.MESH
F32 = jnp.float32
BF16 = jnp.bfloat16
VMEM = pl.BlockSpec(memory_space=pltpu.VMEM)
SMEM = pl.BlockSpec(memory_space=pltpu.SMEM)


def tables(pattern):
    half = pattern // 2
    n = np.arange(half)[:, None]
    out = []
    for parity in (0, 1):
        k = 2 * np.arange(half)[None, :] + parity
        angle = 2.0 * np.pi * ((n * k) % pattern) / pattern
        c, s = np.cos(angle) / np.sqrt(pattern), np.sin(angle) / np.sqrt(pattern)
        full = np.block([[c, -s], [s, c]])
        hi = full.astype(BF16)
        lo = (full - hi.astype(np.float64)).astype(BF16)
        out.append(np.stack([hi, lo]))
    forward = np.stack(out)
    return forward, forward.swapaxes(2, 3)


def reorder_table(pattern):
    half = pattern // 2
    table = np.zeros((pattern, pattern), np.float32)
    table[2 * np.arange(half), np.arange(half)] = 1
    table[2 * np.arange(half) + 1, half + np.arange(half)] = 1
    return table.astype(BF16)


def split(a):
    hi = a.astype(BF16)
    return hi, (a - hi.astype(F32)).astype(BF16)


def times_right(a, table, parity):
    hi, lo = split(a)
    w, v = table[parity, 0], table[parity, 1]
    return jnp.dot(
        jnp.concatenate([hi, lo, hi], axis=1), jnp.concatenate([w, w, v], axis=0), preferred_element_type=F32
    )


def times_left(table, parity, a):
    hi, lo = split(a)
    w, v = table[parity, 0], table[parity, 1]
    return jnp.dot(
        jnp.concatenate([w, w, v], axis=1), jnp.concatenate([hi, lo, hi], axis=0), preferred_element_type=F32
    )


def regroup(a, half):
    re = jnp.concatenate([a[:, :half], a[:, 2 * half : 3 * half]], 1)
    im = jnp.concatenate([a[:, half : 2 * half], a[:, 3 * half :]], 1)
    return jnp.concatenate([re, im], 0)


def reordered_root(measured, order, order_t):
    hi, lo = split(jnp.sqrt(measured))
    root = jnp.dot(hi, order[...], preferred_element_type=F32) + jnp.dot(
        lo, order[...], preferred_element_type=F32
    )
    hi, lo = split(root)
    return jnp.dot(order_t[...], hi, preferred_element_type=F32) + jnp.dot(
        order_t[...], lo, preferred_element_type=F32
    )


def slot_gradient(xr, xi, probe, root, used, forward, backward, factor, add_probe):
    pattern = xr.shape[0]
    half = pattern // 2
    modes = probe.shape[1]
    far = []
    for m in range(modes):
        pr, pi = probe[0, m], probe[1, m]
        wr = pr * xr - pi * xi
        wi = pr * xi + pi * xr
        u = jnp.concatenate([wr[:, :half] + wr[:, half:], wi[:, :half] + wi[:, half:]], 1)
        v = jnp.concatenate([wr[:, :half] - wr[:, half:], wi[:, :half] - wi[:, half:]], 1)
        even = times_right(u, forward, 0)
        odd = times_right(v, forward, 1)
        us = jnp.concatenate([even[:half] + even[half:], odd[:half] + odd[half:]], 1)
        vs = jnp.concatenate([even[:half] - even[half:], odd[:half] - odd[half:]], 1)
        far.append((times_left(backward, 0, regroup(us, half)), times_left(backward, 1, regroup(vs, half))))

    for parity in (0, 1):
        power = 0.0
        for m in range(modes):
            g = far[m][parity]
            power = power + g[:half] * g[:half] + g[half:] * g[half:]
        amplitude = jnp.maximum(jnp.sqrt(power), FLOOR)
        factor[parity] = jnp.where(used, 1.0 - root[parity * half : (parity + 1) * half] / amplitude, 0.0)

    object_r = 0.0
    object_i = 0.0
    for m in range(modes):
        pr, pi = probe[0, m], probe[1, m]
        halves = []
        for parity in (0, 1):
            f = factor[parity]
            g = far[m][parity]
            halves.append(times_left(forward, parity, jnp.concatenate([g[:half] * f, g[half:] * f], 0)))
        top, bottom = halves[0] + halves[1], halves[0] - halves[1]
        k = []
        for parity in (0, 1):
            at = slice(parity * half, (parity + 1) * half)
            z = jnp.concatenate(
                [
                    jnp.concatenate([top[:half, at], top[half:, at]], 1),
                    jnp.concatenate([bottom[:half, at], bottom[half:, at]], 1),
                ],
                0,
            )
            k.append(times_right(z, backward, parity))
        near, off = k[0] + k[1], k[0] - k[1]
        br = jnp.concatenate([near[:, :half], off[:, :half]], 1)
        bi = jnp.concatenate([near[:, half:], off[:, half:]], 1)
        object_r = object_r + pr * br + pi * bi
        object_i = object_i + pr * bi - pi * br
        add_probe(m, xr * br + xi * bi, xr * bi - xi * br)
    return object_r, object_i


def turn(a, amount, axis, unit):
    amount = jnp.broadcast_to(amount, a.shape)
    for k in range(unit.bit_length() - 1):
        a = jnp.where((amount >> k) & 1 == 1, pltpu.roll(a, 1 << k, axis), a)
    return a


def below(shape, axis, amount):
    return lax.broadcasted_iota(jnp.int32, shape, axis) < amount


def rows_in(a, skip):
    a = turn(a, (8 - skip) & 7, 1, 8)
    return jnp.where(below(a[1:].shape, 1, 8 - skip), a[:-1], a[1:])


def rows_out(a, skip):
    a = turn(a, skip, 1, 8)
    zero = jnp.zeros((1,) + a.shape[1:], F32)
    over = jnp.concatenate([zero, a], 0)
    here = jnp.concatenate([a, zero], 0)
    return jnp.where(below(here.shape, 1, skip), over, here)


def cols_in(a, col, half):
    block, rest = lax.div(col, half), lax.rem(col, half)
    a = [a[:, i * half : (i + 1) * half] for i in range(4)]
    block = jnp.broadcast_to(block, a[0].shape)
    blocks = [jnp.where(block == 0, a[i], jnp.where(block == 1, a[i + 1], a[i + 2])) for i in range(2)]
    blocks.append(jnp.where(block == 0, a[2], a[3]))
    blocks = [turn(x, (half - rest) & (half - 1), 1, half) for x in blocks]
    first = below(blocks[0].shape, 1, half - rest)
    return jnp.concatenate([jnp.where(first, blocks[0], blocks[1]), jnp.where(first, blocks[1], blocks[2])], 1)


def cols_out(a, col, half):
    block, rest = lax.div(col, half), lax.rem(col, half)
    blocks = [turn(a[:, i * half : (i + 1) * half], rest, 1, half) for i in range(2)]
    over = below(blocks[0].shape, 1, rest)
    b = [jnp.where(over, 0.0, blocks[0]), jnp.where(over, blocks[0], blocks[1]), jnp.where(over, blocks[1], 0.0)]
    block = jnp.broadcast_to(block, b[0].shape)
    zero, one, two = block == 0, block == 1, block == 2
    return jnp.concatenate(
        [
            jnp.where(zero, b[0], 0.0),
            jnp.where(zero, b[1], jnp.where(one, b[0], 0.0)),
            jnp.where(zero, b[2], jnp.where(one, b[1], b[0])),
            jnp.where(one, b[2], jnp.where(two, b[1], 0.0)),
        ],
        1,
    )


def remote(src, dst, send, recv, ty, tx):
    return pltpu.make_async_remote_copy(
        src_ref=src, dst_ref=dst, send_sem=send, recv_sem=recv, device_id=(ty, tx), device_id_type=MESH
    )


def rows_at(start, size):
    return pl.ds(pl.multiple_of(start, size), size)


def kernel(
    chunks,
    counts, spots, tile, probe_any, measured_any, forward_any, backward_any, order_any, order_t_any,
    inner, total,
    ext, probe, root, forward, backward, order, order_t, factor, placed, part, grid,
    from_below, from_above, side_out, from_side, core_in, plane_in, line_in,
    local, side_send, side_recv, rows_send, rows_recv,
    down_send, down_recv, out_send, out_recv,
    core_send, core_recv, plane_send, plane_recv, line_send, line_recv,
    back_send, back_recv, pair_send, pair_recv,
):
    ty, tx = lax.axis_index("ty"), lax.axis_index("tx")
    n, m = lax.axis_size("ty"), lax.axis_size("tx")
    up, down = lax.rem(ty + n - 1, n), lax.rem(ty + 1, n)
    west, east = lax.rem(tx + m - 1, m), lax.rem(tx + 1, m)
    cells = inner.shape[1]
    margin = cells // 2
    size, far = 2 * cells, cells + margin
    middle = pl.ds(margin, cells)
    edge, inside = margin // 8, cells // 8
    core = lax.rem(ty, 2)
    mate = ty + 1 - 2 * core
    chip, lane, line = ty // 2, lax.rem(tx, 2), tx // 2
    plane_size, line_size = n, m // 2
    me = chip * 2 + lane
    cap = root.shape[0]

    def plane_peer(d):
        other = lax.rem(me + d, plane_size)
        return other, (other // 2) * 2 + core, line * 2 + lax.rem(other, 2)

    def line_peer(d):
        return lax.rem(line + d, line_size) * 2 + lane

    loads = [
        pltpu.make_async_copy(src, dst, local.at[i])
        for i, (src, dst) in enumerate(
            (
                (measured_any.at[0, 0], root),
                (order_any, order),
                (order_t_any, order_t),
                (tile, ext.at[:, pl.ds(edge, inside), :, middle]),
                (probe_any, probe),
                (forward_any, forward),
                (backward_any, backward),
            )
        )
    ]
    for load in loads:
        load.start()

    peers = [(up, tx), (down, tx), (ty, west), (ty, east), (mate, tx)]
    for d in range(1, plane_size):
        peers.append(plane_peer(d)[1:])
    for d in range(1, line_size):
        peers.append((ty, line_peer(d)))
    barrier = pltpu.get_barrier_semaphore()
    for peer in peers:
        pl.semaphore_signal(barrier, inc=1, device_id=peer, device_id_type=MESH)
    pl.semaphore_wait(barrier, len(peers))

    sides = {}
    for step in range(2):
        h = core if step == 0 else 1 - core
        for side, (peer, src, dst) in enumerate(
            ((east, pl.ds(margin, margin), pl.ds(0, margin)), (west, pl.ds(0, margin), pl.ds(far, margin)))
        ):
            copy = remote(
                tile.at[:, pl.ds(h * edge, edge), :, src],
                ext.at[:, pl.ds((h + 1) * edge, edge), :, dst],
                side_send.at[step, side],
                side_recv.at[step, side],
                ty,
                peer,
            )
            copy.start()
            sides[step, side] = copy
    to_up = remote(
        tile.at[:, pl.ds(0, edge)], ext.at[:, pl.ds(3 * edge, edge), :, middle],
        rows_send.at[0, 0], rows_recv.at[0, 0], up, tx,
    )
    to_down = remote(
        tile.at[:, pl.ds(edge, edge)], ext.at[:, pl.ds(0, edge), :, middle],
        rows_send.at[1, 0], rows_recv.at[1, 0], down, tx,
    )
    to_up.start()
    to_down.start()

    placed[...] = jnp.zeros(placed.shape, F32)
    part[...] = jnp.zeros(part.shape, F32)
    ext[:, pl.ds(size // 8, 1)] = jnp.zeros((2, 1, 8, size), F32)
    for load in loads[:3]:
        load.wait()

    @pl.loop(0, cap)
    def _(slot):
        root[slot] = reordered_root(root[slot], order, order_t)

    strips = (pl.ds(0, margin), pl.ds(far, margin))

    def corner(direction, side):
        src, dst, peer = (edge, 3 * edge, up) if direction == 0 else (2 * edge, 0, down)
        return remote(
            ext.at[:, pl.ds(src, edge), :, strips[side]],
            ext.at[:, pl.ds(dst, edge), :, strips[side]],
            rows_send.at[direction, 1 + side],
            rows_recv.at[direction, 1 + side],
            peer,
            tx,
        )

    for step in range(2):
        for side in range(2):
            sides[step, side].wait_recv()
            for direction in range(2):

                @pl.when(core == (direction if step == 0 else 1 - direction))
                def _(direction=direction, side=side):
                    corner(direction, side).start()

    for load in loads[3:]:
        load.wait()
    for copy in sides.values():
        copy.wait_send()
    to_up.wait()
    to_down.wait()
    for direction in range(2):
        for side in range(2):
            corner(direction, side).wait()

    for there, rows, cols in (
        (ty == 0, pl.ds(0, edge), pl.ds(0, size)),
        (ty == n - 1, pl.ds(3 * edge, edge), pl.ds(0, size)),
        (tx == 0, pl.ds(0, size // 8), pl.ds(0, margin)),
        (tx == m - 1, pl.ds(0, size // 8), pl.ds(far, margin)),
    ):

        @pl.when(there)
        def _(rows=rows, cols=cols):
            ext[:, rows, :, cols] = jnp.zeros((2, rows.size, 8, cols.size), F32)

    half = margin
    tall = cells // 8 + 1
    listed = counts[ty, tx]

    def spot(slot):
        row, col = spots[0, 0, slot, 0], spots[0, 0, slot, 1]
        return lax.div(row, 8), lax.rem(row, 8), col

    @pl.loop(0, cap)
    def _(slot):
        group, skip, col = spot(slot)
        used = jnp.broadcast_to(listed, (margin, cells)) > slot

        def window(p):
            strip = ext[p, pl.ds(group, tall)]
            return cols_in(rows_in(strip, skip).reshape(cells, size), col, half)

        def add_probe(mode, re, im):
            for p, value in ((0, re), (1, im)):
                at = pl.ds((p * probe.shape[1] + mode) * cells, cells)
                part[at, :] += value

        pieces = slot_gradient(
            window(0), window(1), probe, root[slot], used, forward, backward, factor, add_probe
        )
        for p, piece in enumerate(pieces):
            piece = cols_out(piece, col, half).reshape(cells // 8, 8, size)
            placed[slot, p, pl.ds(cells // 8, tall)] = rows_out(piece, skip)

    count = part.shape[0] // chunks
    share = count // 2
    piece = share // plane_size
    mine = [c * count + core * share for c in range(chunks)]
    swaps = []
    for c in range(chunks):
        copy = remote(
            part.at[rows_at(c * count + (1 - core) * share, share)],
            core_in.at[c],
            core_send.at[c],
            core_recv.at[c],
            mate,
            tx,
        )
        copy.start()
        swaps.append(copy)

    where = [spot(slot) for slot in range(cap)]

    def assemble(first, height):
        for p in range(2):
            value = 0.0
            for slot, (group, _, _) in enumerate(where):
                value = value + placed[slot, p, pl.ds((cells + first) // 8 - group, height // 8)]
            grid[p, pl.ds(first, height), :] = value.reshape(height, size)

    assemble(0, margin)
    assemble(far, margin)

    row_copies = {}
    cols = (strips[0], strips[1], middle)
    for i, at in enumerate(cols):
        for direction, (src, dst, peer) in enumerate(
            ((pl.ds(0, margin), from_below, up), (pl.ds(far, margin), from_above, down))
        ):
            copy = remote(
                grid.at[:, src, at], dst.at[:, :, at], down_send.at[direction, i], down_recv.at[direction, i], peer, tx
            )
            copy.start()
            row_copies[direction, i] = copy

    plane_copies = []
    for c in range(chunks):
        swaps[c].wait()
        core_in[c] = core_in[c] + part[rows_at(mine[c], share), :]
        copies = []
        for d in range(1, plane_size):
            other, py, px = plane_peer(d)
            copy = remote(
                core_in.at[c, rows_at(other * piece, piece)],
                plane_in.at[c, d],
                plane_send.at[c, d],
                plane_recv.at[c, d],
                py,
                px,
            )
            copy.start()
            copies.append(copy)
        plane_copies.append(copies)

    assemble(margin, cells)

    side_copies = []
    for step in range(2):
        for lower in (True, False):

            @pl.when(core == (0 if lower == (step == 0) else 1))
            def _(lower=lower):
                received = from_below if lower else from_above
                outer = ty == (n - 1 if lower else 0)
                for side in range(2):
                    row_copies[0 if lower else 1, side].wait_recv()
                    at = cols[side]
                    add = jnp.where(outer, 0.0, received[:, :, at])
                    side_out[side, 1 if lower else 0] = grid[:, pl.ds(cells if lower else margin, margin), at] + add

        h = 1 - core if step == 0 else core
        for side, peer in ((0, west), (1, east)):
            copy = remote(
                side_out.at[side, h], from_side.at[side, h], out_send.at[side, step], out_recv.at[side, step], ty, peer
            )
            copy.start()
            side_copies.append(copy)

    line_copies = []
    for c in range(chunks):
        for copy in plane_copies[c]:
            copy.wait()
        own = core_in[c, rows_at(me * piece, piece), :]
        for d in range(1, plane_size):
            own = own + plane_in[c, d]
        line_in[c, line] = own
        copies = []
        for d in range(1, line_size):
            copy = remote(
                line_in.at[c, line], line_in.at[c, line], line_send.at[c, d], line_recv.at[c, d], ty, line_peer(d)
            )
            copy.start()
            copies.append(copy)
        line_copies.append(copies)

    backs, pairs = [], []
    for c in range(chunks):
        for copy in line_copies[c]:
            copy.wait()
        done = line_in[c, 0]
        for d in range(1, line_size):
            done = done + line_in[c, d]
        place = rows_at(mine[c] + me * piece, piece)
        total[place, :] = done * (1.0 / (n * m))
        copies = []
        for d in range(1, plane_size):
            _, py, px = plane_peer(d)
            copy = remote(total.at[place], total.at[place], back_send.at[c, d], back_recv.at[c, d], py, px)
            copy.start()
            copies.append(copy)
        backs.append(copies)
        copy = remote(total.at[place], total.at[place], pair_send.at[c, 0], pair_recv.at[c, 0], mate, tx)
        copy.start()
        pairs.append(copy)

    for direction in range(2):
        row_copies[direction, 2].wait_recv()
    for copy in side_copies:
        copy.wait()
    for h in range(2):
        received = from_above if h == 0 else from_below
        outer = ty == (0 if h == 0 else n - 1)
        value = grid[:, pl.ds((h + 1) * margin, margin), middle] + jnp.where(outer, 0.0, received[:, :, middle])
        from_west = jnp.where(tx == 0, 0.0, from_side[1, h])
        from_east = jnp.where(tx == m - 1, 0.0, from_side[0, h])
        inner[:, pl.ds(h * margin, margin), :] = value + jnp.concatenate([from_west, from_east], 2)
    for copy in row_copies.values():
        copy.wait_send()

    for c in range(chunks):
        for d in range(1, plane_size):
            backs[c][d - 1].wait_recv()
            source = lax.rem(me + plane_size - d, plane_size)
            at = rows_at(mine[c] + source * piece, piece)
            copy = remote(total.at[at], total.at[at], pair_send.at[c, d], pair_recv.at[c, d], mate, tx)
            copy.start()
            pairs.append(copy)
    for copies in backs:
        for copy in copies:
            copy.wait_send()
    for copy in pairs:
        copy.wait()


def shards(object_field, probe_modes, intensities, offsets, counts):
    chunks = 2
    cells = object_field.shape[1]
    margin, size = cells // 2, 2 * cells
    modes = probe_modes.shape[1]
    cap = intensities.shape[2]
    rows = 2 * modes * cells
    plane, line = lax.axis_size("ty"), lax.axis_size("tx") // 2
    share = rows // chunks // 2
    piece = share // plane
    forward, backward = tables(cells)
    order = reorder_table(cells)
    dma = pltpu.SemaphoreType.DMA
    vmem = pltpu.VMEM
    anywhere = pl.BlockSpec(memory_space=pl.ANY)
    inner, total = pl.pallas_call(
        functools.partial(kernel, chunks),
        out_shape=(jax.ShapeDtypeStruct((2, cells, cells), F32), jax.ShapeDtypeStruct((rows, cells), F32)),
        in_specs=[SMEM, SMEM] + [anywhere] * 7,
        out_specs=(VMEM, VMEM),
        scratch_shapes=[
            vmem((2, size // 8 + 1, 8, size), F32),
            vmem(probe_modes.shape, F32),
            vmem((cap, cells, cells), F32),
            vmem(forward.shape, BF16),
            vmem(backward.shape, BF16),
            vmem(order.shape, BF16),
            vmem(order.shape, BF16),
            vmem((2, margin, cells), F32),
            vmem((cap, 2, 3 * cells // 8, 8, size), F32),
            vmem((rows, cells), F32),
            vmem((2, size, size), F32),
            vmem((2, margin, size), F32),
            vmem((2, margin, size), F32),
            vmem((2, 2, 2, margin, margin), F32),
            vmem((2, 2, 2, margin, margin), F32),
            vmem((chunks, share, cells), F32),
            vmem((chunks, plane, piece, cells), F32),
            vmem((chunks, line, piece, cells), F32),
            dma((7,)),
            dma((2, 2)), dma((2, 2)), dma((2, 3)), dma((2, 3)),
            dma((2, 3)), dma((2, 3)), dma((2, 2)), dma((2, 2)),
            dma((chunks,)), dma((chunks,)),
            dma((chunks, plane)), dma((chunks, plane)), dma((chunks, line)), dma((chunks, line)),
            dma((chunks, plane)), dma((chunks, plane)), dma((chunks, plane)), dma((chunks, plane)),
        ],
        compiler_params=pltpu.CompilerParams(collective_id=0, has_side_effects=True),
        name="gradient",
    )(
        counts, offsets, object_field.reshape(2, cells // 8, 8, cells), probe_modes, intensities,
        jnp.asarray(forward), jnp.asarray(backward), jnp.asarray(order), jnp.asarray(order.T),
    )
    return inner, total.reshape(probe_modes.shape)


def solution(mesh):
    placed = (
        P(None, "ty", "tx"),
        P(),
        P("ty", "tx", None, None, None),
        P("ty", "tx", None, None),
        P(),
    )
    return jax.shard_map(
        shards, mesh=mesh, in_specs=placed, out_specs=(P(None, "ty", "tx"), P()), check_vma=False
    )
```

```python
import functools

import jax
import jax.numpy as jnp
import numpy as np
from jax import lax
from jax.experimental import pallas as pl
from jax.experimental.pallas import tpu as pltpu
from jax.sharding import PartitionSpec as P

FLOOR = 0.5
MESH = pl.DeviceIdType.MESH
F32 = jnp.float32
BF16 = jnp.bfloat16
VMEM = pl.BlockSpec(memory_space=pltpu.VMEM)
SMEM = pl.BlockSpec(memory_space=pltpu.SMEM)


def tables(pattern):
    half = pattern // 2
    n = np.arange(half)[:, None]
    out = []
    for parity in (0, 1):
        k = 2 * np.arange(half)[None, :] + parity
        angle = 2.0 * np.pi * ((n * k) % pattern) / pattern
        c, s = np.cos(angle) / np.sqrt(pattern), np.sin(angle) / np.sqrt(pattern)
        full = np.block([[c, -s], [s, c]])
        hi = full.astype(BF16)
        lo = (full - hi.astype(np.float64)).astype(BF16)
        out.append(np.stack([hi, lo]))
    forward = np.stack(out)
    return forward, forward.swapaxes(2, 3)


def reorder_table(pattern):
    half = pattern // 2
    table = np.zeros((pattern, pattern), np.float32)
    table[2 * np.arange(half), np.arange(half)] = 1
    table[2 * np.arange(half) + 1, half + np.arange(half)] = 1
    return table.astype(BF16)


def split(a):
    hi = a.astype(BF16)
    return hi, (a - hi.astype(F32)).astype(BF16)


def times_right(a, table, parity):
    hi, lo = split(a)
    w, v = table[parity, 0], table[parity, 1]
    return jnp.dot(
        jnp.concatenate([hi, lo, hi], axis=1), jnp.concatenate([w, w, v], axis=0), preferred_element_type=F32
    )


def times_left(table, parity, a):
    hi, lo = split(a)
    w, v = table[parity, 0], table[parity, 1]
    return jnp.dot(
        jnp.concatenate([w, w, v], axis=1), jnp.concatenate([hi, lo, hi], axis=0), preferred_element_type=F32
    )


def regroup(a, half):
    re = jnp.concatenate([a[:, :half], a[:, 2 * half : 3 * half]], 1)
    im = jnp.concatenate([a[:, half : 2 * half], a[:, 3 * half :]], 1)
    return jnp.concatenate([re, im], 0)


def reordered_root(measured, order, order_t):
    hi, lo = split(jnp.sqrt(measured))
    root = jnp.dot(hi, order[...], preferred_element_type=F32) + jnp.dot(
        lo, order[...], preferred_element_type=F32
    )
    hi, lo = split(root)
    return jnp.dot(order_t[...], hi, preferred_element_type=F32) + jnp.dot(
        order_t[...], lo, preferred_element_type=F32
    )


def slot_gradient(xr, xi, probe, root, used, forward, backward, factor, add_probe):
    pattern = xr.shape[0]
    half = pattern // 2
    modes = probe.shape[1]
    far = []
    for m in range(modes):
        pr, pi = probe[0, m], probe[1, m]
        wr = pr * xr - pi * xi
        wi = pr * xi + pi * xr
        u = jnp.concatenate([wr[:, :half] + wr[:, half:], wi[:, :half] + wi[:, half:]], 1)
        v = jnp.concatenate([wr[:, :half] - wr[:, half:], wi[:, :half] - wi[:, half:]], 1)
        even = times_right(u, forward, 0)
        odd = times_right(v, forward, 1)
        us = jnp.concatenate([even[:half] + even[half:], odd[:half] + odd[half:]], 1)
        vs = jnp.concatenate([even[:half] - even[half:], odd[:half] - odd[half:]], 1)
        far.append((times_left(backward, 0, regroup(us, half)), times_left(backward, 1, regroup(vs, half))))

    for parity in (0, 1):
        power = 0.0
        for m in range(modes):
            g = far[m][parity]
            power = power + g[:half] * g[:half] + g[half:] * g[half:]
        amplitude = jnp.maximum(jnp.sqrt(power), FLOOR)
        factor[parity] = jnp.where(used, 1.0 - root[parity * half : (parity + 1) * half] / amplitude, 0.0)

    object_r = 0.0
    object_i = 0.0
    for m in range(modes):
        pr, pi = probe[0, m], probe[1, m]
        halves = []
        for parity in (0, 1):
            f = factor[parity]
            g = far[m][parity]
            halves.append(times_left(forward, parity, jnp.concatenate([g[:half] * f, g[half:] * f], 0)))
        top, bottom = halves[0] + halves[1], halves[0] - halves[1]
        k = []
        for parity in (0, 1):
            at = slice(parity * half, (parity + 1) * half)
            z = jnp.concatenate(
                [
                    jnp.concatenate([top[:half, at], top[half:, at]], 1),
                    jnp.concatenate([bottom[:half, at], bottom[half:, at]], 1),
                ],
                0,
            )
            k.append(times_right(z, backward, parity))
        near, off = k[0] + k[1], k[0] - k[1]
        br = jnp.concatenate([near[:, :half], off[:, :half]], 1)
        bi = jnp.concatenate([near[:, half:], off[:, half:]], 1)
        object_r = object_r + pr * br + pi * bi
        object_i = object_i + pr * bi - pi * br
        add_probe(m, xr * br + xi * bi, xr * bi - xi * br)
    return object_r, object_i


def turn(a, amount, axis, unit):
    return pltpu.roll(a, amount, axis)


def below(shape, axis, amount):
    return lax.broadcasted_iota(jnp.int32, shape, axis) < amount


def rows_in(a, skip):
    a = turn(a, (8 - skip) & 7, 1, 8)
    return jnp.where(below(a[1:].shape, 1, 8 - skip), a[:-1], a[1:])


def rows_out(a, skip):
    a = turn(a, skip, 1, 8)
    zero = jnp.zeros((1,) + a.shape[1:], F32)
    over = jnp.concatenate([zero, a], 0)
    here = jnp.concatenate([a, zero], 0)
    return jnp.where(below(here.shape, 1, skip), over, here)


def cols_in(a, col, half):
    block, rest = lax.div(col, half), lax.rem(col, half)
    a = [a[:, i * half : (i + 1) * half] for i in range(4)]
    block = jnp.broadcast_to(block, a[0].shape)
    blocks = [jnp.where(block == 0, a[i], jnp.where(block == 1, a[i + 1], a[i + 2])) for i in range(2)]
    blocks.append(jnp.where(block == 0, a[2], a[3]))
    blocks = [turn(x, (half - rest) & (half - 1), 1, half) for x in blocks]
    first = below(blocks[0].shape, 1, half - rest)
    return jnp.concatenate([jnp.where(first, blocks[0], blocks[1]), jnp.where(first, blocks[1], blocks[2])], 1)


def cols_out(a, col, half):
    block, rest = lax.div(col, half), lax.rem(col, half)
    blocks = [turn(a[:, i * half : (i + 1) * half], rest, 1, half) for i in range(2)]
    over = below(blocks[0].shape, 1, rest)
    b = [jnp.where(over, 0.0, blocks[0]), jnp.where(over, blocks[0], blocks[1]), jnp.where(over, blocks[1], 0.0)]
    block = jnp.broadcast_to(block, b[0].shape)
    zero, one, two = block == 0, block == 1, block == 2
    return jnp.concatenate(
        [
            jnp.where(zero, b[0], 0.0),
            jnp.where(zero, b[1], jnp.where(one, b[0], 0.0)),
            jnp.where(zero, b[2], jnp.where(one, b[1], b[0])),
            jnp.where(one, b[2], jnp.where(two, b[1], 0.0)),
        ],
        1,
    )


def remote(src, dst, send, recv, ty, tx):
    return pltpu.make_async_remote_copy(
        src_ref=src, dst_ref=dst, send_sem=send, recv_sem=recv, device_id=(ty, tx), device_id_type=MESH
    )


def when(there, *steps):
    @pl.when(there)
    def _():
        for step in steps:
            step()


def rows_at(start, size):
    return pl.ds(pl.multiple_of(start, size), size)


def kernel(
    chunks,
    counts_any, spots_any, tile, probe_any, measured_any, forward_any, backward_any, order_any, order_t_any,
    inner, total,
    ext, probe, root, forward, backward, order, order_t, factor, placed, part, grid,
    from_below, from_above, side_out, from_side, core_in, plane_in, line_in,
    pieces_v, counts, spots, local, side_send, side_recv, rows_send, rows_recv,
    down_send, down_recv, out_send, out_recv,
    core_send, core_recv, plane_send, plane_recv, line_send, line_recv,
    back_send, back_recv, pair_send, pair_recv,
):
    ty, tx = lax.axis_index("ty"), lax.axis_index("tx")
    n, m = lax.axis_size("ty"), lax.axis_size("tx")
    up, down = lax.rem(ty + n - 1, n), lax.rem(ty + 1, n)
    west, east = lax.rem(tx + m - 1, m), lax.rem(tx + 1, m)
    cells = inner.shape[1]
    margin = cells // 2
    size, far = 2 * cells, cells + margin
    middle = pl.ds(margin, cells)
    edge, inside = margin // 8, cells // 8
    core = lax.rem(ty, 2)
    mate = ty + 1 - 2 * core
    chip, lane, line = ty // 2, lax.rem(tx, 2), tx // 2
    plane_size, line_size = n, m // 2
    me = chip * 2 + lane
    cap = root.shape[0]
    has_up, has_down, has_west, has_east = ty > 0, ty < n - 1, tx > 0, tx < m - 1

    def plane_peer(d):
        other = lax.rem(me + d, plane_size)
        return other, (other // 2) * 2 + core, line * 2 + lax.rem(other, 2)

    def line_peer(d):
        return lax.rem(line + d, line_size) * 2 + lane

    loads = [
        pltpu.make_async_copy(src, dst, local.at[i])
        for i, (src, dst) in enumerate(
            (
                (measured_any.at[0, 0], root),
                (order_any, order),
                (order_t_any, order_t),
                (tile, ext.at[:, pl.ds(edge, inside), :, middle]),
                (probe_any, probe),
                (forward_any, forward),
                (backward_any, backward),
                (counts_any, counts),
                (spots_any, spots),
            )
        )
    ]
    for load in loads:
        load.start()

    peers = [(up, tx), (down, tx), (ty, west), (ty, east), (mate, tx)]
    for d in range(1, plane_size):
        peers.append(plane_peer(d)[1:])
    for d in range(1, line_size):
        peers.append((ty, line_peer(d)))
    barrier = pltpu.get_barrier_semaphore()
    for peer in peers:
        pl.semaphore_signal(barrier, inc=1, device_id=peer, device_id_type=MESH)
    pl.semaphore_wait(barrier, len(peers))

    sides = {}
    for step in range(2):
        h = core if step == 0 else 1 - core
        for side, (peer, src, dst) in enumerate(
            ((east, pl.ds(margin, margin), pl.ds(0, margin)), (west, pl.ds(0, margin), pl.ds(far, margin)))
        ):
            copy = remote(
                tile.at[:, pl.ds(h * edge, edge), :, src],
                ext.at[:, pl.ds((h + 1) * edge, edge), :, dst],
                side_send.at[step, side],
                side_recv.at[step, side],
                ty,
                peer,
            )
            when(has_east if side == 0 else has_west, copy.start)
            sides[step, side] = copy
    to_up = remote(
        tile.at[:, pl.ds(0, edge)], ext.at[:, pl.ds(3 * edge, edge), :, middle],
        rows_send.at[0, 0], rows_recv.at[0, 0], up, tx,
    )
    to_down = remote(
        tile.at[:, pl.ds(edge, edge)], ext.at[:, pl.ds(0, edge), :, middle],
        rows_send.at[1, 0], rows_recv.at[1, 0], down, tx,
    )
    when(has_up, to_up.start)
    when(has_down, to_down.start)

    placed[...] = jnp.zeros(placed.shape, F32)
    part[...] = jnp.zeros(part.shape, F32)
    ext[:, pl.ds(size // 8, 1)] = jnp.zeros((2, 1, 8, size), F32)
    for there, rows, cols in (
        (has_up, pl.ds(0, edge), pl.ds(0, size)),
        (has_down, pl.ds(3 * edge, edge), pl.ds(0, size)),
        (has_west, pl.ds(0, size // 8), pl.ds(0, margin)),
        (has_east, pl.ds(0, size // 8), pl.ds(far, margin)),
    ):

        @pl.when(jnp.logical_not(there))
        def _(rows=rows, cols=cols):
            ext[:, rows, :, cols] = jnp.zeros((2, rows.size, 8, cols.size), F32)

    for load in loads[:3]:
        load.wait()

    @pl.loop(0, cap)
    def _(slot):
        root[slot] = reordered_root(root[slot], order, order_t)

    strips = (pl.ds(0, margin), pl.ds(far, margin))

    def corner(direction, side):
        src, dst, peer = (edge, 3 * edge, up) if direction == 0 else (2 * edge, 0, down)
        return remote(
            ext.at[:, pl.ds(src, edge), :, strips[side]],
            ext.at[:, pl.ds(dst, edge), :, strips[side]],
            rows_send.at[direction, 1 + side],
            rows_recv.at[direction, 1 + side],
            peer,
            tx,
        )

    has_side, has_row = (has_west, has_east), (has_up, has_down)
    for step in range(2):
        for side in range(2):
            when(has_side[side], sides[step, side].wait_recv)
            for direction in range(2):
                turn_now = core == (direction if step == 0 else 1 - direction)
                when(turn_now & has_side[side] & has_row[direction], corner(direction, side).start)

    for load in loads[3:]:
        load.wait()
    for (_, side), copy in sides.items():
        when(has_side[1 - side], copy.wait_send)
    for direction, copy in ((0, to_up), (1, to_down)):
        when(has_row[direction], copy.wait_send)
        when(has_row[1 - direction], copy.wait_recv)
        for side in range(2):
            when(has_row[direction] & has_side[side], corner(direction, side).wait_send)
            when(has_row[1 - direction] & has_side[side], corner(direction, side).wait_recv)

    half = margin
    tall = cells // 8 + 1
    listed = counts[ty, tx]

    def spot(slot):
        row, col = spots[0, 0, slot, 0], spots[0, 0, slot, 1]
        return lax.div(row, 8), lax.rem(row, 8), col

    @pl.loop(0, cap)
    def _(slot):
        group, skip, col = spot(slot)
        used = jnp.broadcast_to(listed, (margin, cells)) > slot

        def window(p):
            strip = ext[p, pl.ds(group, tall)]
            return cols_in(rows_in(strip, skip).reshape(cells, size), col, half)

        def add_probe(mode, re, im):
            for p, value in ((0, re), (1, im)):
                at = pl.ds((p * probe.shape[1] + mode) * cells, cells)
                part[at, :] += value

        pieces = slot_gradient(
            window(0), window(1), probe, root[slot], used, forward, backward, factor, add_probe
        )
        for p, piece in enumerate(pieces):
            pieces_v[slot, p] = piece

    count = part.shape[0] // chunks
    share = count // 2
    piece = share // plane_size
    mine = [c * count + core * share for c in range(chunks)]
    swaps = []
    for c in range(chunks):
        copy = remote(
            part.at[rows_at(c * count + (1 - core) * share, share)],
            core_in.at[c],
            core_send.at[c],
            core_recv.at[c],
            mate,
            tx,
        )
        copy.start()
        swaps.append(copy)

    @pl.loop(0, cap)
    def _(slot):
        _, skip, col = spot(slot)
        for p in range(2):
            piece = cols_out(pieces_v[slot, p], col, half).reshape(cells // 8, 8, size)
            placed[slot, p, pl.ds(cells // 8, tall)] = rows_out(piece, skip)

    where = [spot(slot) for slot in range(cap)]

    def assemble(first, height):
        for p in range(2):
            value = 0.0
            for slot, (group, _, _) in enumerate(where):
                value = value + placed[slot, p, pl.ds((cells + first) // 8 - group, height // 8)]
            grid[p, pl.ds(first, height), :] = value.reshape(height, size)

    assemble(0, margin)
    assemble(far, margin)

    row_copies = {}
    cols = (strips[0], strips[1], middle)
    for i, at in enumerate(cols):
        for direction, (src, dst, peer) in enumerate(
            ((pl.ds(0, margin), from_below, up), (pl.ds(far, margin), from_above, down))
        ):
            copy = remote(
                grid.at[:, src, at], dst.at[:, :, at], down_send.at[direction, i], down_recv.at[direction, i], peer, tx
            )
            when(has_row[direction], copy.start)
            row_copies[direction, i] = copy

    plane_copies = []
    for c in range(chunks):
        swaps[c].wait()
        core_in[c] = core_in[c] + part[rows_at(mine[c], share), :]
        copies = []
        for d in range(1, plane_size):
            other, py, px = plane_peer(d)
            copy = remote(
                core_in.at[c, rows_at(other * piece, piece)],
                plane_in.at[c, d],
                plane_send.at[c, d],
                plane_recv.at[c, d],
                py,
                px,
            )
            copy.start()
            copies.append(copy)
        plane_copies.append(copies)

    assemble(margin, cells)

    side_copies = []
    for step in range(2):
        for lower in (True, False):

            @pl.when(core == (0 if lower == (step == 0) else 1))
            def _(lower=lower):
                received = from_below if lower else from_above
                outer = jnp.logical_not(has_down if lower else has_up)
                for side in range(2):
                    when(has_down if lower else has_up, row_copies[0 if lower else 1, side].wait_recv)
                    at = cols[side]
                    add = jnp.where(outer, 0.0, received[:, :, at])
                    side_out[side, 1 if lower else 0] = grid[:, pl.ds(cells if lower else margin, margin), at] + add

        h = 1 - core if step == 0 else core
        for side, peer in ((0, west), (1, east)):
            copy = remote(
                side_out.at[side, h], from_side.at[side, h], out_send.at[side, step], out_recv.at[side, step], ty, peer
            )
            when(has_side[side], copy.start)
            side_copies.append((side, copy))

    line_copies = []
    for c in range(chunks):
        for copy in plane_copies[c]:
            copy.wait()
        own = core_in[c, rows_at(me * piece, piece), :]
        for d in range(1, plane_size):
            own = own + plane_in[c, d]
        line_in[c, line] = own
        copies = []
        for d in range(1, line_size):
            copy = remote(
                line_in.at[c, line], line_in.at[c, line], line_send.at[c, d], line_recv.at[c, d], ty, line_peer(d)
            )
            copy.start()
            copies.append(copy)
        line_copies.append(copies)

    backs, pairs = [], []
    for c in range(chunks):
        for copy in line_copies[c]:
            copy.wait()
        done = line_in[c, 0]
        for d in range(1, line_size):
            done = done + line_in[c, d]
        place = rows_at(mine[c] + me * piece, piece)
        total[place, :] = done * (1.0 / (n * m))
        copies = []
        for d in range(1, plane_size):
            _, py, px = plane_peer(d)
            copy = remote(total.at[place], total.at[place], back_send.at[c, d], back_recv.at[c, d], py, px)
            copy.start()
            copies.append(copy)
        backs.append(copies)
        copy = remote(total.at[place], total.at[place], pair_send.at[c, 0], pair_recv.at[c, 0], mate, tx)
        copy.start()
        pairs.append(copy)

    for direction in range(2):
        when(has_row[1 - direction], row_copies[direction, 2].wait_recv)
    for side, copy in side_copies:
        when(has_side[side], copy.wait_send)
        when(has_side[1 - side], copy.wait_recv)
    for h in range(2):
        received = from_above if h == 0 else from_below
        outer = jnp.logical_not(has_up if h == 0 else has_down)
        value = grid[:, pl.ds((h + 1) * margin, margin), middle] + jnp.where(outer, 0.0, received[:, :, middle])
        from_west = jnp.where(has_west, from_side[1, h], 0.0)
        from_east = jnp.where(has_east, from_side[0, h], 0.0)
        inner[:, pl.ds(h * margin, margin), :] = value + jnp.concatenate([from_west, from_east], 2)
    for (direction, _), copy in row_copies.items():
        when(has_row[direction], copy.wait_send)

    for c in range(chunks):
        for d in range(1, plane_size):
            backs[c][d - 1].wait_recv()
            source = lax.rem(me + plane_size - d, plane_size)
            at = rows_at(mine[c] + source * piece, piece)
            copy = remote(total.at[at], total.at[at], pair_send.at[c, d], pair_recv.at[c, d], mate, tx)
            copy.start()
            pairs.append(copy)
    for copies in backs:
        for copy in copies:
            copy.wait_send()
    for copy in pairs:
        copy.wait()


def shards(object_field, probe_modes, intensities, offsets, counts):
    chunks = 2
    cells = object_field.shape[1]
    margin, size = cells // 2, 2 * cells
    modes = probe_modes.shape[1]
    cap = intensities.shape[2]
    rows = 2 * modes * cells
    plane, line = lax.axis_size("ty"), lax.axis_size("tx") // 2
    share = rows // chunks // 2
    piece = share // plane
    forward, backward = tables(cells)
    order = reorder_table(cells)
    dma = pltpu.SemaphoreType.DMA
    vmem = pltpu.VMEM
    anywhere = pl.BlockSpec(memory_space=pltpu.HBM)
    inner, total = pl.pallas_call(
        functools.partial(kernel, chunks),
        out_shape=(jax.ShapeDtypeStruct((2, cells, cells), F32), jax.ShapeDtypeStruct((rows, cells), F32)),
        in_specs=[anywhere] * 9,
        out_specs=(VMEM, VMEM),
        scratch_shapes=[
            vmem((2, size // 8 + 1, 8, size), F32),
            vmem(probe_modes.shape, F32),
            vmem((cap, cells, cells), F32),
            vmem(forward.shape, BF16),
            vmem(backward.shape, BF16),
            vmem(order.shape, BF16),
            vmem(order.shape, BF16),
            vmem((2, margin, cells), F32),
            vmem((cap, 2, 3 * cells // 8, 8, size), F32),
            vmem((rows, cells), F32),
            vmem((2, size, size), F32),
            vmem((2, margin, size), F32),
            vmem((2, margin, size), F32),
            vmem((2, 2, 2, margin, margin), F32),
            vmem((2, 2, 2, margin, margin), F32),
            vmem((chunks, share, cells), F32),
            vmem((chunks, plane, piece, cells), F32),
            vmem((chunks, line, piece, cells), F32),
            vmem((cap, 2, cells, cells), F32),
            pltpu.SMEM((plane, 2 * line), jnp.int32),
            pltpu.SMEM((1, 1, cap, 2), jnp.int32),
            dma((9,)),
            dma((2, 2)), dma((2, 2)), dma((2, 3)), dma((2, 3)),
            dma((2, 3)), dma((2, 3)), dma((2, 2)), dma((2, 2)),
            dma((chunks,)), dma((chunks,)),
            dma((chunks, plane)), dma((chunks, plane)), dma((chunks, line)), dma((chunks, line)),
            dma((chunks, plane)), dma((chunks, plane)), dma((chunks, plane)), dma((chunks, plane)),
        ],
        compiler_params=pltpu.CompilerParams(collective_id=0, has_side_effects=True),
        name="gradient",
    )(
        counts, offsets, object_field.reshape(2, cells // 8, 8, cells), probe_modes, intensities,
        jnp.asarray(forward), jnp.asarray(backward), jnp.asarray(order), jnp.asarray(order.T),
    )
    return inner, total.reshape(probe_modes.shape)


def solution(mesh):
    placed = (
        P(None, "ty", "tx"),
        P(),
        P("ty", "tx", None, None, None),
        P("ty", "tx", None, None),
        P(),
    )
    return jax.shard_map(
        shards, mesh=mesh, in_specs=placed, out_specs=(P(None, "ty", "tx"), P()), check_vma=False
    )
```

```python
import jax
import jax.numpy as jnp
import numpy as np
from jax import lax
from jax.experimental import pallas as pl
from jax.experimental.pallas import tpu as pltpu
from jax.sharding import PartitionSpec as P

FLOOR = 0.5
MESH = pl.DeviceIdType.MESH
F32 = jnp.float32
BF16 = jnp.bfloat16
VMEM = pl.BlockSpec(memory_space=pltpu.VMEM)
SMEM = pl.BlockSpec(memory_space=pltpu.SMEM)


def tables(pattern):
    half = pattern // 2
    n = np.arange(half)[:, None]
    out = []
    for parity in (0, 1):
        k = 2 * np.arange(half)[None, :] + parity
        angle = 2.0 * np.pi * ((n * k) % pattern) / pattern
        c, s = np.cos(angle) / np.sqrt(pattern), np.sin(angle) / np.sqrt(pattern)
        full = np.block([[c, -s], [s, c]])
        hi = full.astype(BF16)
        lo = (full - hi.astype(np.float64)).astype(BF16)
        out.append(np.stack([hi, lo]))
    forward = np.stack(out)
    return forward, forward.swapaxes(2, 3)


def reorder_table(pattern):
    half = pattern // 2
    table = np.zeros((pattern, pattern), np.float32)
    table[2 * np.arange(half), np.arange(half)] = 1
    table[2 * np.arange(half) + 1, half + np.arange(half)] = 1
    return table.astype(BF16)


def split(a):
    hi = a.astype(BF16)
    return hi, (a - hi.astype(F32)).astype(BF16)


def times_right(a, table, parity):
    hi, lo = split(a)
    w, v = table[parity, 0], table[parity, 1]
    return jnp.dot(
        jnp.concatenate([hi, lo, hi], axis=1), jnp.concatenate([w, w, v], axis=0), preferred_element_type=F32
    )


def times_left(table, parity, a):
    hi, lo = split(a)
    w, v = table[parity, 0], table[parity, 1]
    return jnp.dot(
        jnp.concatenate([w, w, v], axis=1), jnp.concatenate([hi, lo, hi], axis=0), preferred_element_type=F32
    )


def regroup(a, half):
    re = jnp.concatenate([a[:, :half], a[:, 2 * half : 3 * half]], 1)
    im = jnp.concatenate([a[:, half : 2 * half], a[:, 3 * half :]], 1)
    return jnp.concatenate([re, im], 0)


def reordered_root(measured, order, order_t):
    hi, lo = split(jnp.sqrt(measured))
    root = jnp.dot(hi, order[...], preferred_element_type=F32) + jnp.dot(
        lo, order[...], preferred_element_type=F32
    )
    hi, lo = split(root)
    return jnp.dot(order_t[...], hi, preferred_element_type=F32) + jnp.dot(
        order_t[...], lo, preferred_element_type=F32
    )


def to_far(xr, xi, probe, root, used, forward, backward, far, factor):
    half = xr.shape[0] // 2
    modes = probe.shape[1]
    power = [0.0, 0.0]
    for m in range(modes):
        pr, pi = probe[0, m], probe[1, m]
        wr = pr * xr - pi * xi
        wi = pr * xi + pi * xr
        u = jnp.concatenate([wr[:, :half] + wr[:, half:], wi[:, :half] + wi[:, half:]], 1)
        v = jnp.concatenate([wr[:, :half] - wr[:, half:], wi[:, :half] - wi[:, half:]], 1)
        even = times_right(u, forward, 0)
        odd = times_right(v, forward, 1)
        us = jnp.concatenate([even[:half] + even[half:], odd[:half] + odd[half:]], 1)
        vs = jnp.concatenate([even[:half] - even[half:], odd[:half] - odd[half:]], 1)
        for parity, x in ((0, us), (1, vs)):
            g = times_left(backward, parity, regroup(x, half))
            far[m, parity] = g
            power[parity] = power[parity] + g[:half] * g[:half] + g[half:] * g[half:]
    for parity in (0, 1):
        amplitude = jnp.maximum(jnp.sqrt(power[parity]), FLOOR)
        factor[parity] = jnp.where(used, 1.0 - root[parity * half : (parity + 1) * half] / amplitude, 0.0)


def from_far(far, factor, forward, backward):
    half = factor.shape[1]
    halves = []
    for parity in (0, 1):
        f, g = factor[parity], far[parity]
        halves.append(times_left(forward, parity, jnp.concatenate([g[:half] * f, g[half:] * f], 0)))
    top, bottom = halves[0] + halves[1], halves[0] - halves[1]
    k = []
    for parity in (0, 1):
        at = slice(parity * half, (parity + 1) * half)
        z = jnp.concatenate(
            [
                jnp.concatenate([top[:half, at], top[half:, at]], 1),
                jnp.concatenate([bottom[:half, at], bottom[half:, at]], 1),
            ],
            0,
        )
        k.append(times_right(z, backward, parity))
    near, off = k[0] + k[1], k[0] - k[1]
    return (
        jnp.concatenate([near[:, :half], off[:, :half]], 1),
        jnp.concatenate([near[:, half:], off[:, half:]], 1),
    )


def turn(a, amount, axis, unit):
    return pltpu.roll(a, amount, axis)


def below(shape, axis, amount):
    return lax.broadcasted_iota(jnp.int32, shape, axis) < amount


def rows_in(a, skip):
    a = turn(a, (8 - skip) & 7, 1, 8)
    return jnp.where(below(a[1:].shape, 1, 8 - skip), a[:-1], a[1:])


def rows_out(a, skip):
    a = turn(a, skip, 1, 8)
    zero = jnp.zeros((1,) + a.shape[1:], F32)
    over = jnp.concatenate([zero, a], 0)
    here = jnp.concatenate([a, zero], 0)
    return jnp.where(below(here.shape, 1, skip), over, here)


def cols_in(a, col, half):
    block, rest = lax.div(col, half), lax.rem(col, half)
    a = [a[:, i * half : (i + 1) * half] for i in range(4)]
    block = jnp.broadcast_to(block, a[0].shape)
    blocks = [jnp.where(block == 0, a[i], jnp.where(block == 1, a[i + 1], a[i + 2])) for i in range(2)]
    blocks.append(jnp.where(block == 0, a[2], a[3]))
    blocks = [turn(x, (half - rest) & (half - 1), 1, half) for x in blocks]
    first = below(blocks[0].shape, 1, half - rest)
    return jnp.concatenate([jnp.where(first, blocks[0], blocks[1]), jnp.where(first, blocks[1], blocks[2])], 1)


def cols_out(a, col, half):
    block, rest = lax.div(col, half), lax.rem(col, half)
    blocks = [turn(a[:, i * half : (i + 1) * half], rest, 1, half) for i in range(2)]
    over = below(blocks[0].shape, 1, rest)
    b = [jnp.where(over, 0.0, blocks[0]), jnp.where(over, blocks[0], blocks[1]), jnp.where(over, blocks[1], 0.0)]
    block = jnp.broadcast_to(block, b[0].shape)
    zero, one, two = block == 0, block == 1, block == 2
    return jnp.concatenate(
        [
            jnp.where(zero, b[0], 0.0),
            jnp.where(zero, b[1], jnp.where(one, b[0], 0.0)),
            jnp.where(zero, b[2], jnp.where(one, b[1], b[0])),
            jnp.where(one, b[2], jnp.where(two, b[1], 0.0)),
        ],
        1,
    )


def remote(src, dst, send, recv, ty, tx):
    return pltpu.make_async_remote_copy(
        src_ref=src, dst_ref=dst, send_sem=send, recv_sem=recv, device_id=(ty, tx), device_id_type=MESH
    )


def when(there, *steps):
    @pl.when(there)
    def _():
        for step in steps:
            step()


def rows_at(start, size):
    return pl.ds(pl.multiple_of(start, size), size)


def kernel(
    counts_any, spots_any, tile, probe_any, measured_any, forward_any, backward_any, order_any, order_t_any,
    inner, total,
    ext, probe, root, forward, backward, order, order_t, factor, placed, part, grid,
    from_below, from_above, side_out, from_side, core_in, plane_in, line_in,
    pieces_v, patch, far_v, counts, spots, local, side_send, side_recv, rows_send, rows_recv,
    down_send, down_recv, out_send, out_recv,
    core_send, core_recv, plane_send, plane_recv, line_send, line_recv,
    back_send, back_recv, pair_send, pair_recv,
):
    ty, tx = lax.axis_index("ty"), lax.axis_index("tx")
    n, m = lax.axis_size("ty"), lax.axis_size("tx")
    up, down = lax.rem(ty + n - 1, n), lax.rem(ty + 1, n)
    west, east = lax.rem(tx + m - 1, m), lax.rem(tx + 1, m)
    cells = inner.shape[1]
    margin = cells // 2
    size, far = 2 * cells, cells + margin
    middle = pl.ds(margin, cells)
    edge, inside = margin // 8, cells // 8
    core = lax.rem(ty, 2)
    mate = ty + 1 - 2 * core
    chip, lane, line = ty // 2, lax.rem(tx, 2), tx // 2
    plane_size, line_size = n, m // 2
    me = chip * 2 + lane
    cap = root.shape[0]
    has_up, has_down, has_west, has_east = ty > 0, ty < n - 1, tx > 0, tx < m - 1

    def plane_peer(d):
        other = lax.rem(me + d, plane_size)
        return other, (other // 2) * 2 + core, line * 2 + lax.rem(other, 2)

    def line_peer(d):
        return lax.rem(line + d, line_size) * 2 + lane

    loads = [
        pltpu.make_async_copy(src, dst, local.at[i])
        for i, (src, dst) in enumerate(
            (
                (measured_any.at[0, 0], root),
                (order_any, order),
                (order_t_any, order_t),
                (tile, ext.at[:, pl.ds(edge, inside), :, middle]),
                (probe_any, probe),
                (forward_any, forward),
                (backward_any, backward),
                (counts_any, counts),
                (spots_any, spots),
            )
        )
    ]
    for load in loads:
        load.start()

    peers = [(up, tx), (down, tx), (ty, west), (ty, east), (mate, tx)]
    for d in range(1, plane_size):
        peers.append(plane_peer(d)[1:])
    for d in range(1, line_size):
        peers.append((ty, line_peer(d)))
    barrier = pltpu.get_barrier_semaphore()
    for peer in peers:
        pl.semaphore_signal(barrier, inc=1, device_id=peer, device_id_type=MESH)
    pl.semaphore_wait(barrier, len(peers))

    sides = {}
    for step in range(2):
        h = core if step == 0 else 1 - core
        for side, (peer, src, dst) in enumerate(
            ((east, pl.ds(margin, margin), pl.ds(0, margin)), (west, pl.ds(0, margin), pl.ds(far, margin)))
        ):
            copy = remote(
                tile.at[:, pl.ds(h * edge, edge), :, src],
                ext.at[:, pl.ds((h + 1) * edge, edge), :, dst],
                side_send.at[step, side],
                side_recv.at[step, side],
                ty,
                peer,
            )
            when(has_east if side == 0 else has_west, copy.start)
            sides[step, side] = copy
    to_up = remote(
        tile.at[:, pl.ds(0, edge)], ext.at[:, pl.ds(3 * edge, edge), :, middle],
        rows_send.at[0, 0], rows_recv.at[0, 0], up, tx,
    )
    to_down = remote(
        tile.at[:, pl.ds(edge, edge)], ext.at[:, pl.ds(0, edge), :, middle],
        rows_send.at[1, 0], rows_recv.at[1, 0], down, tx,
    )
    when(has_up, to_up.start)
    when(has_down, to_down.start)

    placed[...] = jnp.zeros(placed.shape, F32)
    part[...] = jnp.zeros(part.shape, F32)
    ext[:, pl.ds(size // 8, 1)] = jnp.zeros((2, 1, 8, size), F32)
    for there, rows, cols in (
        (has_up, pl.ds(0, edge), pl.ds(0, size)),
        (has_down, pl.ds(3 * edge, edge), pl.ds(0, size)),
        (has_west, pl.ds(0, size // 8), pl.ds(0, margin)),
        (has_east, pl.ds(0, size // 8), pl.ds(far, margin)),
    ):

        @pl.when(jnp.logical_not(there))
        def _(rows=rows, cols=cols):
            ext[:, rows, :, cols] = jnp.zeros((2, rows.size, 8, cols.size), F32)

    for load in loads[:3]:
        load.wait()

    @pl.loop(0, cap)
    def _(slot):
        root[slot] = reordered_root(root[slot], order, order_t)

    strips = (pl.ds(0, margin), pl.ds(far, margin))

    def corner(direction, side):
        src, dst, peer = (edge, 3 * edge, up) if direction == 0 else (2 * edge, 0, down)
        return remote(
            ext.at[:, pl.ds(src, edge), :, strips[side]],
            ext.at[:, pl.ds(dst, edge), :, strips[side]],
            rows_send.at[direction, 1 + side],
            rows_recv.at[direction, 1 + side],
            peer,
            tx,
        )

    has_side, has_row = (has_west, has_east), (has_up, has_down)
    for step in range(2):
        for side in range(2):
            when(has_side[side], sides[step, side].wait_recv)
            for direction in range(2):
                turn_now = core == (direction if step == 0 else 1 - direction)
                when(turn_now & has_side[side] & has_row[direction], corner(direction, side).start)

    for load in loads[3:]:
        load.wait()
    for (_, side), copy in sides.items():
        when(has_side[1 - side], copy.wait_send)
    for direction, copy in ((0, to_up), (1, to_down)):
        when(has_row[direction], copy.wait_send)
        when(has_row[1 - direction], copy.wait_recv)
        for side in range(2):
            when(has_row[direction] & has_side[side], corner(direction, side).wait_send)
            when(has_row[1 - direction] & has_side[side], corner(direction, side).wait_recv)

    half = margin
    tall = cells // 8 + 1
    listed = counts[ty, tx]

    def spot(slot):
        row, col = spots[0, 0, 0, slot], spots[0, 0, 1, slot]
        return lax.div(row, 8), lax.rem(row, 8), col

    @pl.loop(0, cap)
    def _(slot):
        group, skip, col = spot(slot)
        used = jnp.broadcast_to(listed, (margin, cells)) > slot

        def window(p):
            strip = ext[p, pl.ds(group, tall)]
            return cols_in(rows_in(strip, skip).reshape(cells, size), col, half)

        patch[slot, 0], patch[slot, 1] = window(0), window(1)
        to_far(
            patch[slot, 0], patch[slot, 1], probe, root[slot], used, forward, backward,
            far_v.at[slot], factor.at[slot],
        )

    chunks = probe.shape[1]
    count = part.shape[0] // chunks
    share = count // 2
    piece = share // plane_size
    mine = [c * count + core * share for c in range(chunks)]
    swaps, plane_copies = [], []
    for c in range(chunks):
        swaps.append(
            remote(
                part.at[rows_at(c * count + (1 - core) * share, share)],
                core_in.at[c],
                core_send.at[c],
                core_recv.at[c],
                mate,
                tx,
            )
        )
        copies = []
        for d in range(1, plane_size):
            other, py, px = plane_peer(d)
            copies.append(
                remote(
                    core_in.at[c, rows_at(other * piece, piece)],
                    plane_in.at[c, d],
                    plane_send.at[c, d],
                    plane_recv.at[c, d],
                    py,
                    px,
                )
            )
        plane_copies.append(copies)

    def to_plane(c):
        swaps[c].wait()
        core_in[c] = core_in[c] + part[rows_at(mine[c], share), :]
        for copy in plane_copies[c]:
            copy.start()

    for mode in range(chunks):

        @pl.loop(0, cap)
        def _(slot, mode=mode):
            if mode > 0:
                when(slot == cap - 1, lambda: to_plane(mode - 1))
            br, bi = from_far(far_v.at[slot, mode], factor.at[slot], forward, backward)
            xr, xi = patch[slot, 0], patch[slot, 1]
            pr, pi = probe[0, mode], probe[1, mode]
            for p, value in ((0, xr * br + xi * bi), (1, xr * bi - xi * br)):
                part[pl.ds((mode * 2 + p) * cells, cells), :] += value
            for p, value in ((0, pr * br + pi * bi), (1, pr * bi - pi * br)):
                if mode > 0:
                    value = value + pieces_v[slot, p]
                pieces_v[slot, p] = value

        swaps[mode].start()

    @pl.loop(0, cap)
    def _(slot):
        _, skip, col = spot(slot)
        for p in range(2):
            piece = cols_out(pieces_v[slot, p], col, half).reshape(cells // 8, 8, size)
            placed[slot, p, pl.ds(cells // 8, tall)] = rows_out(piece, skip)

    where = [spot(slot) for slot in range(cap)]

    def assemble(first, height):
        for p in range(2):
            value = 0.0
            for slot, (group, _, _) in enumerate(where):
                value = value + placed[slot, p, pl.ds((cells + first) // 8 - group, height // 8)]
            grid[p, pl.ds(first, height), :] = value.reshape(height, size)

    assemble(0, margin)
    assemble(far, margin)
    to_plane(chunks - 1)

    row_copies = {}
    cols = (strips[0], strips[1], middle)
    for i, at in enumerate(cols):
        for direction, (src, dst, peer) in enumerate(
            ((pl.ds(0, margin), from_below, up), (pl.ds(far, margin), from_above, down))
        ):
            copy = remote(
                grid.at[:, src, at], dst.at[:, :, at], down_send.at[direction, i], down_recv.at[direction, i], peer, tx
            )
            when(has_row[direction], copy.start)
            row_copies[direction, i] = copy

    assemble(margin, cells)

    line_copies = []

    def to_line(c):
        for copy in plane_copies[c]:
            copy.wait()
        own = core_in[c, rows_at(me * piece, piece), :]
        for d in range(1, plane_size):
            own = own + plane_in[c, d]
        line_in[c, line] = own
        copies = []
        for d in range(1, line_size):
            copy = remote(
                line_in.at[c, line], line_in.at[c, line], line_send.at[c, d], line_recv.at[c, d], ty, line_peer(d)
            )
            copy.start()
            copies.append(copy)
        line_copies.append(copies)

    side_copies = []
    for step in range(2):
        for lower in (True, False):

            @pl.when(core == (0 if lower == (step == 0) else 1))
            def _(lower=lower):
                received = from_below if lower else from_above
                outer = jnp.logical_not(has_down if lower else has_up)
                for side in range(2):
                    when(has_down if lower else has_up, row_copies[0 if lower else 1, side].wait_recv)
                    at = cols[side]
                    add = jnp.where(outer, 0.0, received[:, :, at])
                    side_out[side, 1 if lower else 0] = grid[:, pl.ds(cells if lower else margin, margin), at] + add

        h = 1 - core if step == 0 else core
        for side, peer in ((0, west), (1, east)):
            copy = remote(
                side_out.at[side, h], from_side.at[side, h], out_send.at[side, step], out_recv.at[side, step], ty, peer
            )
            when(has_side[side], copy.start)
            side_copies.append((side, copy))
        if step == 0:
            to_line(0)
    for c in range(1, chunks):
        to_line(c)

    backs, pairs = [], []
    for c in range(chunks):
        for copy in line_copies[c]:
            copy.wait()
        done = line_in[c, 0]
        for d in range(1, line_size):
            done = done + line_in[c, d]
        place = rows_at(mine[c] + me * piece, piece)
        total[place, :] = done * (1.0 / (n * m))
        copies = []
        for d in range(1, plane_size):
            _, py, px = plane_peer(d)
            copy = remote(total.at[place], total.at[place], back_send.at[c, d], back_recv.at[c, d], py, px)
            copy.start()
            copies.append(copy)
        backs.append(copies)
        copy = remote(total.at[place], total.at[place], pair_send.at[c, 0], pair_recv.at[c, 0], mate, tx)
        copy.start()
        pairs.append(copy)

    for direction in range(2):
        when(has_row[1 - direction], row_copies[direction, 2].wait_recv)
    for side, copy in side_copies:
        when(has_side[side], copy.wait_send)
        when(has_side[1 - side], copy.wait_recv)
    for h in range(2):
        received = from_above if h == 0 else from_below
        outer = jnp.logical_not(has_up if h == 0 else has_down)
        value = grid[:, pl.ds((h + 1) * margin, margin), middle] + jnp.where(outer, 0.0, received[:, :, middle])
        from_west = jnp.where(has_west, from_side[1, h], 0.0)
        from_east = jnp.where(has_east, from_side[0, h], 0.0)
        inner[:, pl.ds(h * margin, margin), :] = value + jnp.concatenate([from_west, from_east], 2)
    for (direction, _), copy in row_copies.items():
        when(has_row[direction], copy.wait_send)

    for c in range(chunks):
        for d in range(1, plane_size):
            backs[c][d - 1].wait_recv()
            source = lax.rem(me + plane_size - d, plane_size)
            at = rows_at(mine[c] + source * piece, piece)
            copy = remote(total.at[at], total.at[at], pair_send.at[c, d], pair_recv.at[c, d], mate, tx)
            copy.start()
            pairs.append(copy)
    for copies in backs:
        for copy in copies:
            copy.wait_send()
    for copy in pairs:
        copy.wait()


def shards(object_field, probe_modes, intensities, offsets, counts):
    cells = object_field.shape[1]
    margin, size = cells // 2, 2 * cells
    modes = chunks = probe_modes.shape[1]
    cap = intensities.shape[2]
    rows = 2 * modes * cells
    plane, line = lax.axis_size("ty"), lax.axis_size("tx") // 2
    share = rows // chunks // 2
    piece = share // plane
    forward, backward = tables(cells)
    order = reorder_table(cells)
    dma = pltpu.SemaphoreType.DMA
    vmem = pltpu.VMEM
    anywhere = pl.BlockSpec(memory_space=pltpu.HBM)
    inner, total = pl.pallas_call(
        kernel,
        out_shape=(jax.ShapeDtypeStruct((2, cells, cells), F32), jax.ShapeDtypeStruct((rows, cells), F32)),
        in_specs=[anywhere] * 9,
        out_specs=(VMEM, VMEM),
        scratch_shapes=[
            vmem((2, size // 8 + 1, 8, size), F32),
            vmem(probe_modes.shape, F32),
            vmem((cap, cells, cells), F32),
            vmem(forward.shape, BF16),
            vmem(backward.shape, BF16),
            vmem(order.shape, BF16),
            vmem(order.shape, BF16),
            vmem((cap, 2, margin, cells), F32),
            vmem((cap, 2, 3 * cells // 8, 8, size), F32),
            vmem((rows, cells), F32),
            vmem((2, size, size), F32),
            vmem((2, margin, size), F32),
            vmem((2, margin, size), F32),
            vmem((2, 2, 2, margin, margin), F32),
            vmem((2, 2, 2, margin, margin), F32),
            vmem((chunks, share, cells), F32),
            vmem((chunks, plane, piece, cells), F32),
            vmem((chunks, line, piece, cells), F32),
            vmem((cap, 2, cells, cells), F32),
            vmem((cap, 2, cells, cells), F32),
            vmem((cap, modes, 2, cells, cells), F32),
            pltpu.SMEM((plane, 2 * line), jnp.int32),
            pltpu.SMEM((1, 1, 2, cap), jnp.int32),
            dma((9,)),
            dma((2, 2)), dma((2, 2)), dma((2, 3)), dma((2, 3)),
            dma((2, 3)), dma((2, 3)), dma((2, 2)), dma((2, 2)),
            dma((chunks,)), dma((chunks,)),
            dma((chunks, plane)), dma((chunks, plane)), dma((chunks, line)), dma((chunks, line)),
            dma((chunks, plane)), dma((chunks, plane)), dma((chunks, plane)), dma((chunks, plane)),
        ],
        compiler_params=pltpu.CompilerParams(collective_id=0, has_side_effects=True, vmem_limit_bytes=44 * 2**20),
        name="gradient",
    )(
        *[
            pltpu.with_memory_space_constraint(x, pltpu.HBM)
            for x in (
                counts,
                offsets.swapaxes(2, 3),
                object_field.reshape(2, cells // 8, 8, cells),
                probe_modes,
                intensities,
                jnp.asarray(forward),
                jnp.asarray(backward),
                jnp.asarray(order),
                jnp.asarray(order.T),
            )
        ]
    )
    return inner, total.reshape(modes, 2, cells, cells).swapaxes(0, 1)


def solution(mesh):
    placed = (
        P(None, "ty", "tx"),
        P(),
        P("ty", "tx", None, None, None),
        P("ty", "tx", None, None),
        P(),
    )
    return jax.shard_map(
        shards, mesh=mesh, in_specs=placed, out_specs=(P(None, "ty", "tx"), P()), check_vma=False
    )
```

```python
import jax
import jax.numpy as jnp
import numpy as np
from jax import lax
from jax.experimental import pallas as pl
from jax.experimental.pallas import tpu as pltpu
from jax.sharding import PartitionSpec as P

FLOOR = 0.5
MESH = pl.DeviceIdType.MESH
F32 = jnp.float32
BF16 = jnp.bfloat16
VMEM = pl.BlockSpec(memory_space=pltpu.VMEM)
SMEM = pl.BlockSpec(memory_space=pltpu.SMEM)


def tables(pattern):
    half = pattern // 2
    n = np.arange(half)[:, None]
    out = []
    for parity in (0, 1):
        k = 2 * np.arange(half)[None, :] + parity
        angle = 2.0 * np.pi * ((n * k) % pattern) / pattern
        c, s = np.cos(angle) / np.sqrt(pattern), np.sin(angle) / np.sqrt(pattern)
        full = np.block([[c, -s], [s, c]])
        hi = full.astype(BF16)
        lo = (full - hi.astype(np.float64)).astype(BF16)
        out.append(np.stack([hi, lo]))
    forward = np.stack(out)
    return forward, forward.swapaxes(2, 3)


def reorder_table(pattern):
    half = pattern // 2
    table = np.zeros((pattern, pattern), np.float32)
    table[2 * np.arange(half), np.arange(half)] = 1
    table[2 * np.arange(half) + 1, half + np.arange(half)] = 1
    return table.astype(BF16)


def split(a):
    hi = a.astype(BF16)
    return hi, (a - hi.astype(F32)).astype(BF16)


def times_right(a, table, parity):
    hi, lo = split(a)
    w, v = table[parity, 0], table[parity, 1]
    return jnp.dot(
        jnp.concatenate([hi, lo, hi], axis=1), jnp.concatenate([w, w, v], axis=0), preferred_element_type=F32
    )


def times_left(table, parity, a):
    hi, lo = split(a)
    w, v = table[parity, 0], table[parity, 1]
    return jnp.dot(
        jnp.concatenate([w, w, v], axis=1), jnp.concatenate([hi, lo, hi], axis=0), preferred_element_type=F32
    )


def regroup(a, half):
    re = jnp.concatenate([a[:, :half], a[:, 2 * half : 3 * half]], 1)
    im = jnp.concatenate([a[:, half : 2 * half], a[:, 3 * half :]], 1)
    return jnp.concatenate([re, im], 0)


def reordered_root(measured, order, order_t):
    hi, lo = split(jnp.sqrt(measured))
    root = jnp.dot(hi, order[...], preferred_element_type=F32) + jnp.dot(
        lo, order[...], preferred_element_type=F32
    )
    hi, lo = split(root)
    return jnp.dot(order_t[...], hi, preferred_element_type=F32) + jnp.dot(
        order_t[...], lo, preferred_element_type=F32
    )


def to_far(xr, xi, probe, root, used, forward, backward, far, factor):
    half = xr.shape[0] // 2
    modes = probe.shape[1]
    power = [0.0, 0.0]
    for m in range(modes):
        pr, pi = probe[0, m], probe[1, m]
        wr = pr * xr - pi * xi
        wi = pr * xi + pi * xr
        u = jnp.concatenate([wr[:, :half] + wr[:, half:], wi[:, :half] + wi[:, half:]], 1)
        v = jnp.concatenate([wr[:, :half] - wr[:, half:], wi[:, :half] - wi[:, half:]], 1)
        even = times_right(u, forward, 0)
        odd = times_right(v, forward, 1)
        us = jnp.concatenate([even[:half] + even[half:], odd[:half] + odd[half:]], 1)
        vs = jnp.concatenate([even[:half] - even[half:], odd[:half] - odd[half:]], 1)
        for parity, x in ((0, us), (1, vs)):
            g = times_left(backward, parity, regroup(x, half))
            far[m, parity] = g
            power[parity] = power[parity] + g[:half] * g[:half] + g[half:] * g[half:]
    for parity in (0, 1):
        amplitude = jnp.maximum(jnp.sqrt(power[parity]), FLOOR)
        factor[parity] = jnp.where(used, 1.0 - root[parity * half : (parity + 1) * half] / amplitude, 0.0)


def from_far(far, factor, forward, backward):
    half = factor.shape[1]
    halves = []
    for parity in (0, 1):
        f, g = factor[parity], far[parity]
        halves.append(times_left(forward, parity, jnp.concatenate([g[:half] * f, g[half:] * f], 0)))
    top, bottom = halves[0] + halves[1], halves[0] - halves[1]
    k = []
    for parity in (0, 1):
        at = slice(parity * half, (parity + 1) * half)
        z = jnp.concatenate(
            [
                jnp.concatenate([top[:half, at], top[half:, at]], 1),
                jnp.concatenate([bottom[:half, at], bottom[half:, at]], 1),
            ],
            0,
        )
        k.append(times_right(z, backward, parity))
    near, off = k[0] + k[1], k[0] - k[1]
    return (
        jnp.concatenate([near[:, :half], off[:, :half]], 1),
        jnp.concatenate([near[:, half:], off[:, half:]], 1),
    )


def turn(a, amount, axis, unit):
    return pltpu.roll(a, amount, axis)


def below(shape, axis, amount):
    return lax.broadcasted_iota(jnp.int32, shape, axis) < amount


def rows_in(a, skip):
    a = turn(a, (8 - skip) & 7, 1, 8)
    return jnp.where(below(a[1:].shape, 1, 8 - skip), a[:-1], a[1:])


def rows_out(a, skip):
    a = turn(a, skip, 1, 8)
    zero = jnp.zeros((1,) + a.shape[1:], F32)
    over = jnp.concatenate([zero, a], 0)
    here = jnp.concatenate([a, zero], 0)
    return jnp.where(below(here.shape, 1, skip), over, here)


def cols_in(a, col, half):
    block, rest = lax.div(col, half), lax.rem(col, half)
    a = [a[:, i * half : (i + 1) * half] for i in range(4)]
    block = jnp.broadcast_to(block, a[0].shape)
    blocks = [jnp.where(block == 0, a[i], jnp.where(block == 1, a[i + 1], a[i + 2])) for i in range(2)]
    blocks.append(jnp.where(block == 0, a[2], a[3]))
    blocks = [turn(x, (half - rest) & (half - 1), 1, half) for x in blocks]
    first = below(blocks[0].shape, 1, half - rest)
    return jnp.concatenate([jnp.where(first, blocks[0], blocks[1]), jnp.where(first, blocks[1], blocks[2])], 1)


def cols_out(a, col, half):
    block, rest = lax.div(col, half), lax.rem(col, half)
    blocks = [turn(a[:, i * half : (i + 1) * half], rest, 1, half) for i in range(2)]
    over = below(blocks[0].shape, 1, rest)
    b = [jnp.where(over, 0.0, blocks[0]), jnp.where(over, blocks[0], blocks[1]), jnp.where(over, blocks[1], 0.0)]
    block = jnp.broadcast_to(block, b[0].shape)
    zero, one, two = block == 0, block == 1, block == 2
    return jnp.concatenate(
        [
            jnp.where(zero, b[0], 0.0),
            jnp.where(zero, b[1], jnp.where(one, b[0], 0.0)),
            jnp.where(zero, b[2], jnp.where(one, b[1], b[0])),
            jnp.where(one, b[2], jnp.where(two, b[1], 0.0)),
        ],
        1,
    )


def remote(src, dst, send, recv, ty, tx):
    return pltpu.make_async_remote_copy(
        src_ref=src, dst_ref=dst, send_sem=send, recv_sem=recv, device_id=(ty, tx), device_id_type=MESH
    )


def when(there, *steps):
    @pl.when(there)
    def _():
        for step in steps:
            step()


def rows_at(start, size):
    return pl.ds(pl.multiple_of(start, size), size)


def kernel(
    counts_any, spots_any, tile, probe_any, measured_any, forward_any, backward_any, order_any, order_t_any,
    inner, total,
    ext, probe, root, forward, backward, order, order_t, factor, placed, part, grid,
    from_below, from_above, side_out, from_side, core_in, plane_in, line_in,
    pieces_v, patch, far_v, counts, spots, local, side_send, side_recv, rows_send, rows_recv,
    down_send, down_recv, out_send, out_recv,
    core_send, core_recv, plane_send, plane_recv, line_send, line_recv,
    back_send, back_recv, pair_send, pair_recv,
):
    ty, tx = lax.axis_index("ty"), lax.axis_index("tx")
    n, m = lax.axis_size("ty"), lax.axis_size("tx")
    up, down = lax.rem(ty + n - 1, n), lax.rem(ty + 1, n)
    west, east = lax.rem(tx + m - 1, m), lax.rem(tx + 1, m)
    cells = inner.shape[1]
    margin = cells // 2
    size, far = 2 * cells, cells + margin
    middle = pl.ds(margin, cells)
    edge, inside = margin // 8, cells // 8
    core = lax.rem(ty, 2)
    mate = ty + 1 - 2 * core
    chip, lane, line = ty // 2, lax.rem(tx, 2), tx // 2
    plane_size, line_size = n, m // 2
    me = chip * 2 + lane
    cap = root.shape[0]
    has_up, has_down, has_west, has_east = ty > 0, ty < n - 1, tx > 0, tx < m - 1

    def plane_peer(d):
        other = lax.rem(me + d, plane_size)
        return other, (other // 2) * 2 + core, line * 2 + lax.rem(other, 2)

    def line_peer(d):
        return lax.rem(line + d, line_size) * 2 + lane

    loads = [
        pltpu.make_async_copy(src, dst, local.at[i])
        for i, (src, dst) in enumerate(
            (
                (measured_any.at[0, 0], root),
                (order_any, order),
                (order_t_any, order_t),
                (tile, ext.at[:, pl.ds(edge, inside), :, middle]),
                (probe_any, probe),
                (forward_any, forward),
                (backward_any, backward),
                (counts_any, counts),
                (spots_any, spots),
            )
        )
    ]
    for load in loads:
        load.start()

    peers = [(up, tx), (down, tx), (ty, west), (ty, east), (mate, tx)]
    for d in range(1, plane_size):
        peers.append(plane_peer(d)[1:])
    for d in range(1, line_size):
        peers.append((ty, line_peer(d)))
    barrier = pltpu.get_barrier_semaphore()
    for peer in peers:
        pl.semaphore_signal(barrier, inc=1, device_id=peer, device_id_type=MESH)
    pl.semaphore_wait(barrier, len(peers))

    sides = {}
    for step in range(2):
        h = core if step == 0 else 1 - core
        for side, (peer, src, dst) in enumerate(
            ((east, pl.ds(margin, margin), pl.ds(0, margin)), (west, pl.ds(0, margin), pl.ds(far, margin)))
        ):
            copy = remote(
                tile.at[:, pl.ds(h * edge, edge), :, src],
                ext.at[:, pl.ds((h + 1) * edge, edge), :, dst],
                side_send.at[step, side],
                side_recv.at[step, side],
                ty,
                peer,
            )
            when(has_east if side == 0 else has_west, copy.start)
            sides[step, side] = copy
    to_up = remote(
        tile.at[:, pl.ds(0, edge)], ext.at[:, pl.ds(3 * edge, edge), :, middle],
        rows_send.at[0, 0], rows_recv.at[0, 0], up, tx,
    )
    to_down = remote(
        tile.at[:, pl.ds(edge, edge)], ext.at[:, pl.ds(0, edge), :, middle],
        rows_send.at[1, 0], rows_recv.at[1, 0], down, tx,
    )
    when(has_up, to_up.start)
    when(has_down, to_down.start)

    placed[...] = jnp.zeros(placed.shape, F32)
    part[...] = jnp.zeros(part.shape, F32)
    ext[:, pl.ds(size // 8, 1)] = jnp.zeros((2, 1, 8, size), F32)
    for there, rows, cols in (
        (has_up, pl.ds(0, edge), pl.ds(0, size)),
        (has_down, pl.ds(3 * edge, edge), pl.ds(0, size)),
        (has_west, pl.ds(0, size // 8), pl.ds(0, margin)),
        (has_east, pl.ds(0, size // 8), pl.ds(far, margin)),
    ):

        @pl.when(jnp.logical_not(there))
        def _(rows=rows, cols=cols):
            ext[:, rows, :, cols] = jnp.zeros((2, rows.size, 8, cols.size), F32)

    for load in loads[:3]:
        load.wait()

    @pl.loop(0, cap)
    def _(slot):
        root[slot] = reordered_root(root[slot], order, order_t)

    strips = (pl.ds(0, margin), pl.ds(far, margin))

    def corner(direction, side):
        src, dst, peer = (edge, 3 * edge, up) if direction == 0 else (2 * edge, 0, down)
        return remote(
            ext.at[:, pl.ds(src, edge), :, strips[side]],
            ext.at[:, pl.ds(dst, edge), :, strips[side]],
            rows_send.at[direction, 1 + side],
            rows_recv.at[direction, 1 + side],
            peer,
            tx,
        )

    has_side, has_row = (has_west, has_east), (has_up, has_down)
    for step in range(2):
        for side in range(2):
            when(has_side[side], sides[step, side].wait_recv)
            for direction in range(2):
                turn_now = core == (direction if step == 0 else 1 - direction)
                when(turn_now & has_side[side] & has_row[direction], corner(direction, side).start)

    for load in loads[3:]:
        load.wait()
    for (_, side), copy in sides.items():
        when(has_side[1 - side], copy.wait_send)
    for direction, copy in ((0, to_up), (1, to_down)):
        when(has_row[direction], copy.wait_send)
        when(has_row[1 - direction], copy.wait_recv)
        for side in range(2):
            when(has_row[direction] & has_side[side], corner(direction, side).wait_send)
            when(has_row[1 - direction] & has_side[side], corner(direction, side).wait_recv)

    half = margin
    tall = cells // 8 + 1
    listed = counts[ty, tx]

    def spot(slot):
        row, col = spots[0, 0, 0, slot], spots[0, 0, 1, slot]
        return lax.div(row, 8), lax.rem(row, 8), col

    @pl.loop(0, cap)
    def _(slot):
        group, skip, col = spot(slot)
        used = jnp.broadcast_to(listed, (margin, cells)) > slot

        def window(p):
            strip = ext[p, pl.ds(group, tall)]
            return cols_in(rows_in(strip, skip).reshape(cells, size), col, half)

        patch[slot, 0], patch[slot, 1] = window(0), window(1)
        to_far(
            patch[slot, 0], patch[slot, 1], probe, root[slot], used, forward, backward,
            far_v.at[slot], factor.at[slot],
        )

    chunks = probe.shape[1]
    count = part.shape[0] // chunks
    share = count // 2
    piece = share // plane_size
    mine = [c * count + core * share for c in range(chunks)]
    swaps, plane_copies = [], []
    for c in range(chunks):
        swaps.append(
            remote(
                part.at[rows_at(c * count + (1 - core) * share, share)],
                core_in.at[c],
                core_send.at[c],
                core_recv.at[c],
                mate,
                tx,
            )
        )
        copies = []
        for d in range(1, plane_size):
            other, py, px = plane_peer(d)
            copies.append(
                remote(
                    core_in.at[c, rows_at(other * piece, piece)],
                    plane_in.at[c, d],
                    plane_send.at[c, d],
                    plane_recv.at[c, d],
                    py,
                    px,
                )
            )
        plane_copies.append(copies)

    def to_plane(c):
        swaps[c].wait()
        core_in[c] = core_in[c] + part[rows_at(mine[c], share), :]
        for copy in plane_copies[c]:
            copy.start()

    for mode in range(chunks):

        @pl.loop(0, cap)
        def _(slot, mode=mode):
            if mode > 0:
                when(slot == cap - 1, lambda: to_plane(mode - 1))
            br, bi = from_far(far_v.at[slot, mode], factor.at[slot], forward, backward)
            xr, xi = patch[slot, 0], patch[slot, 1]
            pr, pi = probe[0, mode], probe[1, mode]
            for p, value in ((0, xr * br + xi * bi), (1, xr * bi - xi * br)):
                part[pl.ds((mode * 2 + p) * cells, cells), :] += value
            for p, value in ((0, pr * br + pi * bi), (1, pr * bi - pi * br)):
                if mode > 0:
                    value = value + pieces_v[slot, p]
                pieces_v[slot, p] = value

        swaps[mode].start()

    @pl.loop(0, cap)
    def _(slot):
        _, skip, col = spot(slot)
        for p in range(2):
            piece = cols_out(pieces_v[slot, p], col, half).reshape(cells // 8, 8, size)
            placed[slot, p, pl.ds(cells // 8, tall)] = rows_out(piece, skip)

    where = [spot(slot) for slot in range(cap)]

    def assemble(first, height):
        for p in range(2):
            value = 0.0
            for slot, (group, _, _) in enumerate(where):
                value = value + placed[slot, p, pl.ds((cells + first) // 8 - group, height // 8)]
            grid[p, pl.ds(first, height), :] = value.reshape(height, size)

    assemble(0, margin)
    assemble(far, margin)
    to_plane(chunks - 1)

    row_copies = {}
    cols = (strips[0], strips[1], middle)
    for i, at in enumerate(cols):
        for direction, (src, dst, peer) in enumerate(
            ((pl.ds(0, margin), from_below, up), (pl.ds(far, margin), from_above, down))
        ):
            copy = remote(
                grid.at[:, src, at], dst.at[:, :, at], down_send.at[direction, i], down_recv.at[direction, i], peer, tx
            )
            when(has_row[direction], copy.start)
            row_copies[direction, i] = copy

    assemble(margin, cells)

    line_copies = []

    def to_line(c):
        for copy in plane_copies[c]:
            copy.wait()
        own = core_in[c, rows_at(me * piece, piece), :]
        for d in range(1, plane_size):
            own = own + plane_in[c, d]
        line_in[c, line] = own
        copies = []
        for d in range(1, line_size):
            copy = remote(
                line_in.at[c, line], line_in.at[c, line], line_send.at[c, d], line_recv.at[c, d], ty, line_peer(d)
            )
            copy.start()
            copies.append(copy)
        line_copies.append(copies)

    side_copies = []

    def to_sides(step):
        for lower in (True, False):

            @pl.when(core == (0 if lower == (step == 0) else 1))
            def _(lower=lower):
                received = from_below if lower else from_above
                outer = jnp.logical_not(has_down if lower else has_up)
                for side in range(2):
                    when(has_down if lower else has_up, row_copies[0 if lower else 1, side].wait_recv)
                    at = cols[side]
                    add = jnp.where(outer, 0.0, received[:, :, at])
                    side_out[side, 1 if lower else 0] = grid[:, pl.ds(cells if lower else margin, margin), at] + add

        h = 1 - core if step == 0 else core
        for side, peer in ((0, west), (1, east)):
            copy = remote(
                side_out.at[side, h], from_side.at[side, h], out_send.at[side, step], out_recv.at[side, step], ty, peer
            )
            when(has_side[side], copy.start)
            side_copies.append((side, copy))

    to_sides(0)
    to_line(0)
    to_line(1)
    to_sides(1)

    backs, pairs = [], []
    for c in range(chunks):
        for copy in line_copies[c]:
            copy.wait()
        done = line_in[c, 0]
        for d in range(1, line_size):
            done = done + line_in[c, d]
        place = rows_at(mine[c] + me * piece, piece)
        total[place, :] = done * (1.0 / (n * m))
        copies = []
        for d in range(1, plane_size):
            _, py, px = plane_peer(d)
            copy = remote(total.at[place], total.at[place], back_send.at[c, d], back_recv.at[c, d], py, px)
            copy.start()
            copies.append(copy)
        backs.append(copies)
        copy = remote(total.at[place], total.at[place], pair_send.at[c, 0], pair_recv.at[c, 0], mate, tx)
        copy.start()
        pairs.append(copy)

    for direction in range(2):
        when(has_row[1 - direction], row_copies[direction, 2].wait_recv)
    for side, copy in side_copies:
        when(has_side[side], copy.wait_send)
        when(has_side[1 - side], copy.wait_recv)
    for h in range(2):
        received = from_above if h == 0 else from_below
        outer = jnp.logical_not(has_up if h == 0 else has_down)
        value = grid[:, pl.ds((h + 1) * margin, margin), middle] + jnp.where(outer, 0.0, received[:, :, middle])
        from_west = jnp.where(has_west, from_side[1, h], 0.0)
        from_east = jnp.where(has_east, from_side[0, h], 0.0)
        inner[:, pl.ds(h * margin, margin), :] = value + jnp.concatenate([from_west, from_east], 2)
    for (direction, _), copy in row_copies.items():
        when(has_row[direction], copy.wait_send)

    for c in range(chunks):
        for d in range(1, plane_size):
            backs[c][d - 1].wait_recv()
            source = lax.rem(me + plane_size - d, plane_size)
            at = rows_at(mine[c] + source * piece, piece)
            copy = remote(total.at[at], total.at[at], pair_send.at[c, d], pair_recv.at[c, d], mate, tx)
            copy.start()
            pairs.append(copy)
    for copies in backs:
        for copy in copies:
            copy.wait_send()
    for copy in pairs:
        copy.wait()


def shards(object_field, probe_modes, intensities, offsets, counts):
    cells = object_field.shape[1]
    margin, size = cells // 2, 2 * cells
    modes = chunks = probe_modes.shape[1]
    cap = intensities.shape[2]
    rows = 2 * modes * cells
    plane, line = lax.axis_size("ty"), lax.axis_size("tx") // 2
    share = rows // chunks // 2
    piece = share // plane
    forward, backward = tables(cells)
    order = reorder_table(cells)
    dma = pltpu.SemaphoreType.DMA
    vmem = pltpu.VMEM
    anywhere = pl.BlockSpec(memory_space=pltpu.HBM)
    inner, total = pl.pallas_call(
        kernel,
        out_shape=(jax.ShapeDtypeStruct((2, cells, cells), F32), jax.ShapeDtypeStruct((rows, cells), F32)),
        in_specs=[anywhere] * 9,
        out_specs=(VMEM, VMEM),
        scratch_shapes=[
            vmem((2, size // 8 + 1, 8, size), F32),
            vmem(probe_modes.shape, F32),
            vmem((cap, cells, cells), F32),
            vmem(forward.shape, BF16),
            vmem(backward.shape, BF16),
            vmem(order.shape, BF16),
            vmem(order.shape, BF16),
            vmem((cap, 2, margin, cells), F32),
            vmem((cap, 2, 3 * cells // 8, 8, size), F32),
            vmem((rows, cells), F32),
            vmem((2, size, size), F32),
            vmem((2, margin, size), F32),
            vmem((2, margin, size), F32),
            vmem((2, 2, 2, margin, margin), F32),
            vmem((2, 2, 2, margin, margin), F32),
            vmem((chunks, share, cells), F32),
            vmem((chunks, plane, piece, cells), F32),
            vmem((chunks, line, piece, cells), F32),
            vmem((cap, 2, cells, cells), F32),
            vmem((cap, 2, cells, cells), F32),
            vmem((cap, modes, 2, cells, cells), F32),
            pltpu.SMEM((plane, 2 * line), jnp.int32),
            pltpu.SMEM((1, 1, 2, cap), jnp.int32),
            dma((9,)),
            dma((2, 2)), dma((2, 2)), dma((2, 3)), dma((2, 3)),
            dma((2, 3)), dma((2, 3)), dma((2, 2)), dma((2, 2)),
            dma((chunks,)), dma((chunks,)),
            dma((chunks, plane)), dma((chunks, plane)), dma((chunks, line)), dma((chunks, line)),
            dma((chunks, plane)), dma((chunks, plane)), dma((chunks, plane)), dma((chunks, plane)),
        ],
        compiler_params=pltpu.CompilerParams(collective_id=0, has_side_effects=True, vmem_limit_bytes=44 * 2**20),
        name="gradient",
    )(
        *[
            pltpu.with_memory_space_constraint(x, pltpu.HBM)
            for x in (
                counts,
                offsets.swapaxes(2, 3),
                object_field.reshape(2, cells // 8, 8, cells),
                probe_modes,
                intensities,
                jnp.asarray(forward),
                jnp.asarray(backward),
                jnp.asarray(order),
                jnp.asarray(order.T),
            )
        ]
    )
    return inner, total.reshape(modes, 2, cells, cells).swapaxes(0, 1)


def solution(mesh):
    placed = (
        P(None, "ty", "tx"),
        P(),
        P("ty", "tx", None, None, None),
        P("ty", "tx", None, None),
        P(),
    )
    return jax.shard_map(
        shards, mesh=mesh, in_specs=placed, out_specs=(P(None, "ty", "tx"), P()), check_vma=False
    )
```

```python
import jax
import jax.numpy as jnp
import numpy as np
from jax import lax
from jax.experimental import pallas as pl
from jax.experimental.pallas import tpu as pltpu
from jax.sharding import PartitionSpec as P

FLOOR = 0.5
MESH = pl.DeviceIdType.MESH
F32 = jnp.float32
BF16 = jnp.bfloat16
VMEM = pl.BlockSpec(memory_space=pltpu.VMEM)
SMEM = pl.BlockSpec(memory_space=pltpu.SMEM)


def tables(pattern):
    half = pattern // 2
    n = np.arange(half)[:, None]
    out = []
    for parity in (0, 1):
        k = 2 * np.arange(half)[None, :] + parity
        angle = 2.0 * np.pi * ((n * k) % pattern) / pattern
        c, s = np.cos(angle) / np.sqrt(pattern), np.sin(angle) / np.sqrt(pattern)
        full = np.block([[c, -s], [s, c]])
        hi = full.astype(BF16)
        lo = (full - hi.astype(np.float64)).astype(BF16)
        out.append(np.stack([hi, lo]))
    forward = np.stack(out)
    return forward, forward.swapaxes(2, 3)


def reorder_table(pattern):
    half = pattern // 2
    table = np.zeros((pattern, pattern), np.float32)
    table[2 * np.arange(half), np.arange(half)] = 1
    table[2 * np.arange(half) + 1, half + np.arange(half)] = 1
    return table.astype(BF16)


def split(a):
    hi = a.astype(BF16)
    return hi, (a - hi.astype(F32)).astype(BF16)


def times_right(a, table, parity):
    hi, lo = split(a)
    w, v = table[parity, 0], table[parity, 1]
    return jnp.dot(
        jnp.concatenate([hi, lo, hi], axis=1), jnp.concatenate([w, w, v], axis=0), preferred_element_type=F32
    )


def times_left(table, parity, a):
    hi, lo = split(a)
    w, v = table[parity, 0], table[parity, 1]
    return jnp.dot(
        jnp.concatenate([w, w, v], axis=1), jnp.concatenate([hi, lo, hi], axis=0), preferred_element_type=F32
    )


def regroup(a, half):
    re = jnp.concatenate([a[:, :half], a[:, 2 * half : 3 * half]], 1)
    im = jnp.concatenate([a[:, half : 2 * half], a[:, 3 * half :]], 1)
    return jnp.concatenate([re, im], 0)


def reordered_root(measured, order, order_t):
    hi, lo = split(jnp.sqrt(measured))
    root = jnp.dot(hi, order[...], preferred_element_type=F32) + jnp.dot(
        lo, order[...], preferred_element_type=F32
    )
    hi, lo = split(root)
    return jnp.dot(order_t[...], hi, preferred_element_type=F32) + jnp.dot(
        order_t[...], lo, preferred_element_type=F32
    )


def to_far(xr, xi, probe, root, used, forward, backward, far, factor):
    half = xr.shape[0] // 2
    modes = probe.shape[1]
    power = [0.0, 0.0]
    for m in range(modes):
        pr, pi = probe[0, m], probe[1, m]
        wr = pr * xr - pi * xi
        wi = pr * xi + pi * xr
        u = jnp.concatenate([wr[:, :half] + wr[:, half:], wi[:, :half] + wi[:, half:]], 1)
        v = jnp.concatenate([wr[:, :half] - wr[:, half:], wi[:, :half] - wi[:, half:]], 1)
        even = times_right(u, forward, 0)
        odd = times_right(v, forward, 1)
        us = jnp.concatenate([even[:half] + even[half:], odd[:half] + odd[half:]], 1)
        vs = jnp.concatenate([even[:half] - even[half:], odd[:half] - odd[half:]], 1)
        for parity, x in ((0, us), (1, vs)):
            g = times_left(backward, parity, regroup(x, half))
            far[m, parity] = g
            power[parity] = power[parity] + g[:half] * g[:half] + g[half:] * g[half:]
    for parity in (0, 1):
        amplitude = jnp.maximum(jnp.sqrt(power[parity]), FLOOR)
        factor[parity] = jnp.where(used, 1.0 - root[parity * half : (parity + 1) * half] / amplitude, 0.0)


def from_far(far, factor, forward, backward):
    half = factor.shape[1]
    halves = []
    for parity in (0, 1):
        f, g = factor[parity], far[parity]
        halves.append(times_left(forward, parity, jnp.concatenate([g[:half] * f, g[half:] * f], 0)))
    top, bottom = halves[0] + halves[1], halves[0] - halves[1]
    k = []
    for parity in (0, 1):
        at = slice(parity * half, (parity + 1) * half)
        z = jnp.concatenate(
            [
                jnp.concatenate([top[:half, at], top[half:, at]], 1),
                jnp.concatenate([bottom[:half, at], bottom[half:, at]], 1),
            ],
            0,
        )
        k.append(times_right(z, backward, parity))
    near, off = k[0] + k[1], k[0] - k[1]
    return (
        jnp.concatenate([near[:, :half], off[:, :half]], 1),
        jnp.concatenate([near[:, half:], off[:, half:]], 1),
    )


def turn(a, amount, axis, unit):
    return pltpu.roll(a, amount, axis)


def below(shape, axis, amount):
    return lax.broadcasted_iota(jnp.int32, shape, axis) < amount


def rows_in(a, skip):
    a = turn(a, (8 - skip) & 7, 1, 8)
    return jnp.where(below(a[1:].shape, 1, 8 - skip), a[:-1], a[1:])


def rows_out(a, skip):
    a = turn(a, skip, 1, 8)
    zero = jnp.zeros((1,) + a.shape[1:], F32)
    over = jnp.concatenate([zero, a], 0)
    here = jnp.concatenate([a, zero], 0)
    return jnp.where(below(here.shape, 1, skip), over, here)


def cols_in(a, col, half):
    block, rest = lax.div(col, half), lax.rem(col, half)
    a = [a[:, i * half : (i + 1) * half] for i in range(4)]
    block = jnp.broadcast_to(block, a[0].shape)
    blocks = [jnp.where(block == 0, a[i], jnp.where(block == 1, a[i + 1], a[i + 2])) for i in range(2)]
    blocks.append(jnp.where(block == 0, a[2], a[3]))
    blocks = [turn(x, (half - rest) & (half - 1), 1, half) for x in blocks]
    first = below(blocks[0].shape, 1, half - rest)
    return jnp.concatenate([jnp.where(first, blocks[0], blocks[1]), jnp.where(first, blocks[1], blocks[2])], 1)


def cols_out(a, col, half):
    block, rest = lax.div(col, half), lax.rem(col, half)
    blocks = [turn(a[:, i * half : (i + 1) * half], rest, 1, half) for i in range(2)]
    over = below(blocks[0].shape, 1, rest)
    b = [jnp.where(over, 0.0, blocks[0]), jnp.where(over, blocks[0], blocks[1]), jnp.where(over, blocks[1], 0.0)]
    block = jnp.broadcast_to(block, b[0].shape)
    zero, one, two = block == 0, block == 1, block == 2
    return jnp.concatenate(
        [
            jnp.where(zero, b[0], 0.0),
            jnp.where(zero, b[1], jnp.where(one, b[0], 0.0)),
            jnp.where(zero, b[2], jnp.where(one, b[1], b[0])),
            jnp.where(one, b[2], jnp.where(two, b[1], 0.0)),
        ],
        1,
    )


def remote(src, dst, send, recv, ty, tx):
    return pltpu.make_async_remote_copy(
        src_ref=src, dst_ref=dst, send_sem=send, recv_sem=recv, device_id=(ty, tx), device_id_type=MESH
    )


def when(there, *steps):
    @pl.when(there)
    def _():
        for step in steps:
            step()


def rows_at(start, size):
    return pl.ds(pl.multiple_of(start, size), size)


def kernel(
    counts_any, spots_any, tile, probe_any, measured_any, forward_any, backward_any, order_any, order_t_any,
    inner, total,
    ext, probe, root, forward, backward, order, order_t, factor, placed, part, grid,
    from_below, from_above, side_out, from_side, core_in, plane_in, line_in,
    pieces_v, patch, far_v, counts, spots, local, side_send, side_recv, rows_send, rows_recv,
    down_send, down_recv, out_send, out_recv,
    core_send, core_recv, plane_send, plane_recv, line_send, line_recv,
    back_send, back_recv, pair_send, pair_recv,
):
    ty, tx = lax.axis_index("ty"), lax.axis_index("tx")
    n, m = lax.axis_size("ty"), lax.axis_size("tx")
    up, down = lax.rem(ty + n - 1, n), lax.rem(ty + 1, n)
    west, east = lax.rem(tx + m - 1, m), lax.rem(tx + 1, m)
    cells = inner.shape[1]
    margin = cells // 2
    size, far = 2 * cells, cells + margin
    middle = pl.ds(margin, cells)
    edge, inside = margin // 8, cells // 8
    core = lax.rem(ty, 2)
    mate = ty + 1 - 2 * core
    chip, lane, line = ty // 2, lax.rem(tx, 2), tx // 2
    plane_size, line_size = n, m // 2
    me = chip * 2 + lane
    cap = root.shape[0]
    has_up, has_down, has_west, has_east = ty > 0, ty < n - 1, tx > 0, tx < m - 1

    def plane_peer(d):
        other = lax.rem(me + d, plane_size)
        return other, (other // 2) * 2 + core, line * 2 + lax.rem(other, 2)

    def line_peer(d):
        return lax.rem(line + d, line_size) * 2 + lane

    loads = [
        pltpu.make_async_copy(src, dst, local.at[i])
        for i, (src, dst) in enumerate(
            (
                (measured_any.at[0, 0], root),
                (order_any, order),
                (order_t_any, order_t),
                (tile, ext.at[:, pl.ds(edge, inside), :, middle]),
                (probe_any, probe),
                (forward_any, forward),
                (backward_any, backward),
                (counts_any, counts),
                (spots_any, spots),
            )
        )
    ]
    for load in loads:
        load.start()

    peers = [(up, tx), (down, tx), (ty, west), (ty, east), (mate, tx)]
    peers += [(up, west), (up, east), (down, west), (down, east)]
    for d in range(1, plane_size):
        peers.append(plane_peer(d)[1:])
    for d in range(1, line_size):
        peers.append((ty, line_peer(d)))
    barrier = pltpu.get_barrier_semaphore()
    for peer in peers:
        pl.semaphore_signal(barrier, inc=1, device_id=peer, device_id_type=MESH)
    placed[...] = jnp.zeros(placed.shape, F32)
    part[...] = jnp.zeros(part.shape, F32)
    ext[:, pl.ds(size // 8, 1)] = jnp.zeros((2, 1, 8, size), F32)
    for there, rows, cols in (
        (has_up, pl.ds(0, edge), pl.ds(0, size)),
        (has_down, pl.ds(3 * edge, edge), pl.ds(0, size)),
        (has_west, pl.ds(0, size // 8), pl.ds(0, margin)),
        (has_east, pl.ds(0, size // 8), pl.ds(far, margin)),
    ):

        @pl.when(jnp.logical_not(there))
        def _(rows=rows, cols=cols):
            ext[:, rows, :, cols] = jnp.zeros((2, rows.size, 8, cols.size), F32)

    for load in loads[:3]:
        load.wait()

    @pl.loop(0, cap)
    def _(slot):
        root[slot] = reordered_root(root[slot], order, order_t)

    pl.semaphore_wait(barrier, len(peers))

    sides = {}
    for step in range(2):
        h = core if step == 0 else 1 - core
        for side, (peer, src, dst) in enumerate(
            ((east, pl.ds(margin, margin), pl.ds(0, margin)), (west, pl.ds(0, margin), pl.ds(far, margin)))
        ):
            copy = remote(
                tile.at[:, pl.ds(h * edge, edge), :, src],
                ext.at[:, pl.ds((h + 1) * edge, edge), :, dst],
                side_send.at[step, side],
                side_recv.at[step, side],
                ty,
                peer,
            )
            when(has_east if side == 0 else has_west, copy.start)
            sides[step, side] = copy
    to_up = remote(
        tile.at[:, pl.ds(0, edge)], ext.at[:, pl.ds(3 * edge, edge), :, middle],
        rows_send.at[0, 0], rows_recv.at[0, 0], up, tx,
    )
    to_down = remote(
        tile.at[:, pl.ds(edge, edge)], ext.at[:, pl.ds(0, edge), :, middle],
        rows_send.at[1, 0], rows_recv.at[1, 0], down, tx,
    )
    when(has_up, to_up.start)
    when(has_down, to_down.start)

    has_side, has_row = (has_west, has_east), (has_up, has_down)
    across = (lax.rem(ty, n // 2) == 0, lax.rem(ty, n // 2) == n // 2 - 1)
    strips = (pl.ds(0, margin), pl.ds(far, margin))

    def straight(direction, side):
        src, dst, row = (0, 3 * edge, up) if direction == 0 else (edge, 0, down)
        return remote(
            tile.at[:, pl.ds(src, edge), :, pl.ds(margin if side == 0 else 0, margin)],
            ext.at[:, pl.ds(dst, edge), :, strips[side]],
            rows_send.at[direction, 1 + side],
            rows_recv.at[direction, 1 + side],
            row,
            east if side == 0 else west,
        )

    for direction in range(2):
        for side in range(2):
            when(across[direction] & has_row[direction] & has_side[1 - side], straight(direction, side).start)

    def corner(direction, side):
        src, dst, peer = (edge, 3 * edge, up) if direction == 0 else (2 * edge, 0, down)
        return remote(
            ext.at[:, pl.ds(src, edge), :, strips[side]],
            ext.at[:, pl.ds(dst, edge), :, strips[side]],
            rows_send.at[direction, 1 + side],
            rows_recv.at[direction, 1 + side],
            peer,
            tx,
        )

    for step in range(2):
        for side in range(2):
            when(has_side[side], sides[step, side].wait_recv)
            for direction in range(2):
                turn_now = core == (direction if step == 0 else 1 - direction)
                near = jnp.logical_not(across[direction])
                when(turn_now & near & has_side[side] & has_row[direction], corner(direction, side).start)

    for load in loads[3:]:
        load.wait()
    for (_, side), copy in sides.items():
        when(has_side[1 - side], copy.wait_send)
    for direction, copy in ((0, to_up), (1, to_down)):
        when(has_row[direction], copy.wait_send)
        when(has_row[1 - direction], copy.wait_recv)
        for side in range(2):
            near = jnp.logical_not(across[direction])
            when(near & has_row[direction] & has_side[side], corner(direction, side).wait_send)
            when(across[direction] & has_row[direction] & has_side[1 - side], straight(direction, side).wait_send)
            when(has_row[1 - direction] & has_side[side], corner(direction, side).wait_recv)

    half = margin
    tall = cells // 8 + 1
    listed = counts[ty, tx]

    def spot(slot):
        row, col = spots[0, 0, 0, slot], spots[0, 0, 1, slot]
        return lax.div(row, 8), lax.rem(row, 8), col

    @pl.loop(0, cap)
    def _(slot):
        group, skip, col = spot(slot)
        used = jnp.broadcast_to(listed, (margin, cells)) > slot

        def window(p):
            strip = ext[p, pl.ds(group, tall)]
            return cols_in(rows_in(strip, skip).reshape(cells, size), col, half)

        patch[slot, 0], patch[slot, 1] = window(0), window(1)
        to_far(
            patch[slot, 0], patch[slot, 1], probe, root[slot], used, forward, backward,
            far_v.at[slot], factor.at[slot],
        )

    chunks = probe.shape[1]
    count = part.shape[0] // chunks
    share = count // 2
    piece = share // plane_size
    mine = [c * count + core * share for c in range(chunks)]
    swaps, plane_copies = [], []
    for c in range(chunks):
        swaps.append(
            remote(
                part.at[rows_at(c * count + (1 - core) * share, share)],
                core_in.at[c],
                core_send.at[c],
                core_recv.at[c],
                mate,
                tx,
            )
        )
        copies = []
        for d in range(1, plane_size):
            other, py, px = plane_peer(d)
            copies.append(
                remote(
                    core_in.at[c, rows_at(other * piece, piece)],
                    plane_in.at[c, d],
                    plane_send.at[c, d],
                    plane_recv.at[c, d],
                    py,
                    px,
                )
            )
        plane_copies.append(copies)

    def to_plane(c):
        swaps[c].wait()
        core_in[c] = core_in[c] + part[rows_at(mine[c], share), :]
        for copy in plane_copies[c]:
            copy.start()

    for mode in range(chunks):

        @pl.loop(0, cap)
        def _(slot, mode=mode):
            if mode > 0:
                when(slot == cap - 1, lambda: to_plane(mode - 1))
            br, bi = from_far(far_v.at[slot, mode], factor.at[slot], forward, backward)
            xr, xi = patch[slot, 0], patch[slot, 1]
            pr, pi = probe[0, mode], probe[1, mode]
            for p, value in ((0, xr * br + xi * bi), (1, xr * bi - xi * br)):
                part[pl.ds((mode * 2 + p) * cells, cells), :] += value
            for p, value in ((0, pr * br + pi * bi), (1, pr * bi - pi * br)):
                if mode > 0:
                    value = value + pieces_v[slot, p]
                pieces_v[slot, p] = value

        swaps[mode].start()

    @pl.loop(0, cap)
    def _(slot):
        _, skip, col = spot(slot)
        for p in range(2):
            piece = cols_out(pieces_v[slot, p], col, half).reshape(cells // 8, 8, size)
            placed[slot, p, pl.ds(cells // 8, tall)] = rows_out(piece, skip)

    where = [spot(slot) for slot in range(cap)]

    def assemble(first, height):
        for p in range(2):
            value = 0.0
            for slot, (group, _, _) in enumerate(where):
                value = value + placed[slot, p, pl.ds((cells + first) // 8 - group, height // 8)]
            grid[p, pl.ds(first, height), :] = value.reshape(height, size)

    assemble(0, margin)
    assemble(far, margin)
    to_plane(chunks - 1)

    row_copies = {}
    cols = (strips[0], strips[1], middle)
    for i, at in enumerate(cols):
        for direction, (src, dst, peer) in enumerate(
            ((pl.ds(0, margin), from_below, up), (pl.ds(far, margin), from_above, down))
        ):
            copy = remote(
                grid.at[:, src, at], dst.at[:, :, at], down_send.at[direction, i], down_recv.at[direction, i], peer, tx
            )
            if i < 2:
                when(has_row[direction], copy.start)
            row_copies[direction, i] = copy

    assemble(margin, cells)

    line_copies = []

    def to_line(c):
        for copy in plane_copies[c]:
            copy.wait()
        own = core_in[c, rows_at(me * piece, piece), :]
        for d in range(1, plane_size):
            own = own + plane_in[c, d]
        line_in[c, line] = own
        copies = []
        for d in range(1, line_size):
            copy = remote(
                line_in.at[c, line], line_in.at[c, line], line_send.at[c, d], line_recv.at[c, d], ty, line_peer(d)
            )
            copy.start()
            copies.append(copy)
        line_copies.append(copies)

    side_copies = []

    def to_sides(step):
        for lower in (True, False):

            @pl.when(core == (0 if lower == (step == 0) else 1))
            def _(lower=lower):
                received = from_below if lower else from_above
                outer = jnp.logical_not(has_down if lower else has_up)
                for side in range(2):
                    when(has_down if lower else has_up, row_copies[0 if lower else 1, side].wait_recv)
                    at = cols[side]
                    add = jnp.where(outer, 0.0, received[:, :, at])
                    side_out[side, 1 if lower else 0] = grid[:, pl.ds(cells if lower else margin, margin), at] + add

        h = 1 - core if step == 0 else core
        for side, peer in ((0, west), (1, east)):
            copy = remote(
                side_out.at[side, h], from_side.at[side, h], out_send.at[side, step], out_recv.at[side, step], ty, peer
            )
            when(has_side[side], copy.start)
            side_copies.append((side, copy))

    to_sides(0)
    to_line(0)
    to_line(1)
    for direction in range(2):
        when(has_row[direction], row_copies[direction, 2].start)
    to_sides(1)

    backs, pairs = [], []
    for c in range(chunks):
        for copy in line_copies[c]:
            copy.wait()
        done = line_in[c, 0]
        for d in range(1, line_size):
            done = done + line_in[c, d]
        place = rows_at(mine[c] + me * piece, piece)
        total[place, :] = done * (1.0 / (n * m))
        copies = []
        for d in range(1, plane_size):
            _, py, px = plane_peer(d)
            copy = remote(total.at[place], total.at[place], back_send.at[c, d], back_recv.at[c, d], py, px)
            copy.start()
            copies.append(copy)
        backs.append(copies)
        copy = remote(total.at[place], total.at[place], pair_send.at[c, 0], pair_recv.at[c, 0], mate, tx)
        copy.start()
        pairs.append(copy)

    for direction in range(2):
        when(has_row[1 - direction], row_copies[direction, 2].wait_recv)
    for side, copy in side_copies:
        when(has_side[side], copy.wait_send)
        when(has_side[1 - side], copy.wait_recv)
    for h in range(2):
        received = from_above if h == 0 else from_below
        outer = jnp.logical_not(has_up if h == 0 else has_down)
        value = grid[:, pl.ds((h + 1) * margin, margin), middle] + jnp.where(outer, 0.0, received[:, :, middle])
        from_west = jnp.where(has_west, from_side[1, h], 0.0)
        from_east = jnp.where(has_east, from_side[0, h], 0.0)
        inner[:, pl.ds(h * margin, margin), :] = value + jnp.concatenate([from_west, from_east], 2)
    for (direction, _), copy in row_copies.items():
        when(has_row[direction], copy.wait_send)

    for c in range(chunks):
        for d in range(1, plane_size):
            backs[c][d - 1].wait_recv()
            source = lax.rem(me + plane_size - d, plane_size)
            at = rows_at(mine[c] + source * piece, piece)
            copy = remote(total.at[at], total.at[at], pair_send.at[c, d], pair_recv.at[c, d], mate, tx)
            copy.start()
            pairs.append(copy)
    for copies in backs:
        for copy in copies:
            copy.wait_send()
    for copy in pairs:
        copy.wait()


def shards(object_field, probe_modes, intensities, offsets, counts):
    cells = object_field.shape[1]
    margin, size = cells // 2, 2 * cells
    modes = chunks = probe_modes.shape[1]
    cap = intensities.shape[2]
    rows = 2 * modes * cells
    plane, line = lax.axis_size("ty"), lax.axis_size("tx") // 2
    share = rows // chunks // 2
    piece = share // plane
    forward, backward = tables(cells)
    order = reorder_table(cells)
    dma = pltpu.SemaphoreType.DMA
    vmem = pltpu.VMEM
    anywhere = pl.BlockSpec(memory_space=pltpu.HBM)
    inner, total = pl.pallas_call(
        kernel,
        out_shape=(jax.ShapeDtypeStruct((2, cells, cells), F32), jax.ShapeDtypeStruct((rows, cells), F32)),
        in_specs=[anywhere] * 9,
        out_specs=(VMEM, VMEM),
        scratch_shapes=[
            vmem((2, size // 8 + 1, 8, size), F32),
            vmem(probe_modes.shape, F32),
            vmem((cap, cells, cells), F32),
            vmem(forward.shape, BF16),
            vmem(backward.shape, BF16),
            vmem(order.shape, BF16),
            vmem(order.shape, BF16),
            vmem((cap, 2, margin, cells), F32),
            vmem((cap, 2, 3 * cells // 8, 8, size), F32),
            vmem((rows, cells), F32),
            vmem((2, size, size), F32),
            vmem((2, margin, size), F32),
            vmem((2, margin, size), F32),
            vmem((2, 2, 2, margin, margin), F32),
            vmem((2, 2, 2, margin, margin), F32),
            vmem((chunks, share, cells), F32),
            vmem((chunks, plane, piece, cells), F32),
            vmem((chunks, line, piece, cells), F32),
            vmem((cap, 2, cells, cells), F32),
            vmem((cap, 2, cells, cells), F32),
            vmem((cap, modes, 2, cells, cells), F32),
            pltpu.SMEM((plane, 2 * line), jnp.int32),
            pltpu.SMEM((1, 1, 2, cap), jnp.int32),
            dma((9,)),
            dma((2, 2)), dma((2, 2)), dma((2, 3)), dma((2, 3)),
            dma((2, 3)), dma((2, 3)), dma((2, 2)), dma((2, 2)),
            dma((chunks,)), dma((chunks,)),
            dma((chunks, plane)), dma((chunks, plane)), dma((chunks, line)), dma((chunks, line)),
            dma((chunks, plane)), dma((chunks, plane)), dma((chunks, plane)), dma((chunks, plane)),
        ],
        compiler_params=pltpu.CompilerParams(collective_id=0, has_side_effects=True, vmem_limit_bytes=44 * 2**20),
        name="gradient",
    )(
        *[
            pltpu.with_memory_space_constraint(x, pltpu.HBM)
            for x in (
                counts,
                offsets.swapaxes(2, 3),
                object_field.reshape(2, cells // 8, 8, cells),
                probe_modes,
                intensities,
                jnp.asarray(forward),
                jnp.asarray(backward),
                jnp.asarray(order),
                jnp.asarray(order.T),
            )
        ]
    )
    return inner, total.reshape(modes, 2, cells, cells).swapaxes(0, 1)


def solution(mesh):
    placed = (
        P(None, "ty", "tx"),
        P(),
        P("ty", "tx", None, None, None),
        P("ty", "tx", None, None),
        P(),
    )
    return jax.shard_map(
        shards, mesh=mesh, in_specs=placed, out_specs=(P(None, "ty", "tx"), P()), check_vma=False
    )
```

```python
import jax
import jax.numpy as jnp
import numpy as np
from jax import lax
from jax.experimental import pallas as pl
from jax.experimental.pallas import tpu as pltpu
from jax.sharding import PartitionSpec as P

FLOOR = 0.5
MESH = pl.DeviceIdType.MESH
F32 = jnp.float32
BF16 = jnp.bfloat16
VMEM = pl.BlockSpec(memory_space=pltpu.VMEM)
SMEM = pl.BlockSpec(memory_space=pltpu.SMEM)


def tables(pattern):
    half = pattern // 2
    n = np.arange(half)[:, None]
    out = []
    for parity in (0, 1):
        k = 2 * np.arange(half)[None, :] + parity
        angle = 2.0 * np.pi * ((n * k) % pattern) / pattern
        c, s = np.cos(angle) / np.sqrt(pattern), np.sin(angle) / np.sqrt(pattern)
        full = np.block([[c, -s], [s, c]])
        hi = full.astype(BF16)
        lo = (full - hi.astype(np.float64)).astype(BF16)
        out.append(np.stack([hi, lo]))
    forward = np.stack(out)
    return forward, forward.swapaxes(2, 3)


def reorder_table(pattern):
    half = pattern // 2
    table = np.zeros((pattern, pattern), np.float32)
    table[2 * np.arange(half), np.arange(half)] = 1
    table[2 * np.arange(half) + 1, half + np.arange(half)] = 1
    return table.astype(BF16)


def split(a):
    hi = a.astype(BF16)
    return hi, (a - hi.astype(F32)).astype(BF16)


def times_right(a, table, parity):
    hi, lo = split(a)
    w, v = table[parity, 0], table[parity, 1]
    return jnp.dot(
        jnp.concatenate([hi, lo, hi], axis=1), jnp.concatenate([w, w, v], axis=0), preferred_element_type=F32
    )


def times_left(table, parity, a):
    hi, lo = split(a)
    w, v = table[parity, 0], table[parity, 1]
    return jnp.dot(
        jnp.concatenate([w, w, v], axis=1), jnp.concatenate([hi, lo, hi], axis=0), preferred_element_type=F32
    )


def regroup(a, half):
    re = jnp.concatenate([a[:, :half], a[:, 2 * half : 3 * half]], 1)
    im = jnp.concatenate([a[:, half : 2 * half], a[:, 3 * half :]], 1)
    return jnp.concatenate([re, im], 0)


def reordered_root(measured, order, order_t):
    hi, lo = split(jnp.sqrt(measured))
    root = jnp.dot(hi, order[...], preferred_element_type=F32) + jnp.dot(
        lo, order[...], preferred_element_type=F32
    )
    hi, lo = split(root)
    return jnp.dot(order_t[...], hi, preferred_element_type=F32) + jnp.dot(
        order_t[...], lo, preferred_element_type=F32
    )


def to_far(xr, xi, probe, root, used, forward, backward, far, factor):
    half = xr.shape[0] // 2
    modes = probe.shape[1]
    power = [0.0, 0.0]
    for m in range(modes):
        pr, pi = probe[0, m], probe[1, m]
        wr = pr * xr - pi * xi
        wi = pr * xi + pi * xr
        u = jnp.concatenate([wr[:, :half] + wr[:, half:], wi[:, :half] + wi[:, half:]], 1)
        v = jnp.concatenate([wr[:, :half] - wr[:, half:], wi[:, :half] - wi[:, half:]], 1)
        even = times_right(u, forward, 0)
        odd = times_right(v, forward, 1)
        us = jnp.concatenate([even[:half] + even[half:], odd[:half] + odd[half:]], 1)
        vs = jnp.concatenate([even[:half] - even[half:], odd[:half] - odd[half:]], 1)
        for parity, x in ((0, us), (1, vs)):
            g = times_left(backward, parity, regroup(x, half))
            far[m, parity] = g
            power[parity] = power[parity] + g[:half] * g[:half] + g[half:] * g[half:]
    for parity in (0, 1):
        amplitude = jnp.maximum(jnp.sqrt(power[parity]), FLOOR)
        factor[parity] = jnp.where(used, 1.0 - root[parity * half : (parity + 1) * half] / amplitude, 0.0)


def from_far(far, factor, forward, backward):
    half = factor.shape[1]
    halves = []
    for parity in (0, 1):
        f, g = factor[parity], far[parity]
        halves.append(times_left(forward, parity, jnp.concatenate([g[:half] * f, g[half:] * f], 0)))
    top, bottom = halves[0] + halves[1], halves[0] - halves[1]
    k = []
    for parity in (0, 1):
        at = slice(parity * half, (parity + 1) * half)
        z = jnp.concatenate(
            [
                jnp.concatenate([top[:half, at], top[half:, at]], 1),
                jnp.concatenate([bottom[:half, at], bottom[half:, at]], 1),
            ],
            0,
        )
        k.append(times_right(z, backward, parity))
    near, off = k[0] + k[1], k[0] - k[1]
    return (
        jnp.concatenate([near[:, :half], off[:, :half]], 1),
        jnp.concatenate([near[:, half:], off[:, half:]], 1),
    )


def turn(a, amount, axis, unit):
    return pltpu.roll(a, amount, axis)


def below(shape, axis, amount):
    return lax.broadcasted_iota(jnp.int32, shape, axis) < amount


def rows_in(a, skip):
    a = turn(a, (8 - skip) & 7, 1, 8)
    return jnp.where(below(a[1:].shape, 1, 8 - skip), a[:-1], a[1:])


def rows_out(a, skip):
    a = turn(a, skip, 1, 8)
    zero = jnp.zeros((1,) + a.shape[1:], F32)
    over = jnp.concatenate([zero, a], 0)
    here = jnp.concatenate([a, zero], 0)
    return jnp.where(below(here.shape, 1, skip), over, here)


def cols_in(a, col, half):
    block, rest = lax.div(col, half), lax.rem(col, half)
    a = [a[:, i * half : (i + 1) * half] for i in range(4)]
    block = jnp.broadcast_to(block, a[0].shape)
    blocks = [jnp.where(block == 0, a[i], jnp.where(block == 1, a[i + 1], a[i + 2])) for i in range(2)]
    blocks.append(jnp.where(block == 0, a[2], a[3]))
    blocks = [turn(x, (half - rest) & (half - 1), 1, half) for x in blocks]
    first = below(blocks[0].shape, 1, half - rest)
    return jnp.concatenate([jnp.where(first, blocks[0], blocks[1]), jnp.where(first, blocks[1], blocks[2])], 1)


def cols_out(a, col, half):
    block, rest = lax.div(col, half), lax.rem(col, half)
    blocks = [turn(a[:, i * half : (i + 1) * half], rest, 1, half) for i in range(2)]
    over = below(blocks[0].shape, 1, rest)
    b = [jnp.where(over, 0.0, blocks[0]), jnp.where(over, blocks[0], blocks[1]), jnp.where(over, blocks[1], 0.0)]
    block = jnp.broadcast_to(block, b[0].shape)
    zero, one, two = block == 0, block == 1, block == 2
    return jnp.concatenate(
        [
            jnp.where(zero, b[0], 0.0),
            jnp.where(zero, b[1], jnp.where(one, b[0], 0.0)),
            jnp.where(zero, b[2], jnp.where(one, b[1], b[0])),
            jnp.where(one, b[2], jnp.where(two, b[1], 0.0)),
        ],
        1,
    )


def remote(src, dst, send, recv, ty, tx):
    return pltpu.make_async_remote_copy(
        src_ref=src, dst_ref=dst, send_sem=send, recv_sem=recv, device_id=(ty, tx), device_id_type=MESH
    )


def when(there, *steps):
    @pl.when(there)
    def _():
        for step in steps:
            step()


def rows_at(start, size):
    return pl.ds(pl.multiple_of(start, size), size)


def kernel(
    counts_any, spots_any, tile, probe_any, measured_any, forward_any, backward_any, order_any, order_t_any,
    inner, total,
    ext, probe, root, forward, backward, order, order_t, factor, placed, part, grid,
    from_below, from_above, side_out, from_side, core_in, plane_in, line_in,
    pieces_v, patch, far_v, counts, spots, local, side_send, side_recv, rows_send, rows_recv,
    down_send, down_recv, out_send, out_recv,
    core_send, core_recv, plane_send, plane_recv, line_send, line_recv,
    back_send, back_recv, pair_send, pair_recv,
):
    ty, tx = lax.axis_index("ty"), lax.axis_index("tx")
    n, m = lax.axis_size("ty"), lax.axis_size("tx")
    up, down = lax.rem(ty + n - 1, n), lax.rem(ty + 1, n)
    west, east = lax.rem(tx + m - 1, m), lax.rem(tx + 1, m)
    cells = inner.shape[1]
    margin = cells // 2
    size, far = 2 * cells, cells + margin
    middle = pl.ds(margin, cells)
    edge, inside = margin // 8, cells // 8
    core = lax.rem(ty, 2)
    mate = ty + 1 - 2 * core
    chip, lane, line = ty // 2, lax.rem(tx, 2), tx // 2
    plane_size, line_size = n, m // 2
    me = chip * 2 + lane
    cap = root.shape[0]
    has_up, has_down, has_west, has_east = ty > 0, ty < n - 1, tx > 0, tx < m - 1

    def plane_peer(d):
        other = lax.rem(me + d, plane_size)
        return other, (other // 2) * 2 + core, line * 2 + lax.rem(other, 2)

    def line_peer(d):
        return lax.rem(line + d, line_size) * 2 + lane

    loads = [
        pltpu.make_async_copy(src, dst, local.at[i])
        for i, (src, dst) in enumerate(
            (
                (measured_any.at[0, 0], root),
                (order_any, order),
                (order_t_any, order_t),
                (tile, ext.at[:, pl.ds(edge, inside), :, middle]),
                (probe_any, probe),
                (forward_any, forward),
                (backward_any, backward),
                (counts_any, counts),
                (spots_any, spots),
            )
        )
    ]
    for load in loads:
        load.start()

    peers = [(up, tx), (down, tx), (ty, west), (ty, east), (mate, tx)]
    peers += [(up, west), (up, east), (down, west), (down, east)]
    for d in range(1, plane_size):
        peers.append(plane_peer(d)[1:])
    for d in range(1, line_size):
        peers.append((ty, line_peer(d)))
    barrier = pltpu.get_barrier_semaphore()
    for peer in peers:
        pl.semaphore_signal(barrier, inc=1, device_id=peer, device_id_type=MESH)
    placed[...] = jnp.zeros(placed.shape, F32)
    part[...] = jnp.zeros(part.shape, F32)
    ext[:, pl.ds(size // 8, 1)] = jnp.zeros((2, 1, 8, size), F32)
    for there, rows, cols in (
        (has_up, pl.ds(0, edge), pl.ds(0, size)),
        (has_down, pl.ds(3 * edge, edge), pl.ds(0, size)),
        (has_west, pl.ds(0, size // 8), pl.ds(0, margin)),
        (has_east, pl.ds(0, size // 8), pl.ds(far, margin)),
    ):

        @pl.when(jnp.logical_not(there))
        def _(rows=rows, cols=cols):
            ext[:, rows, :, cols] = jnp.zeros((2, rows.size, 8, cols.size), F32)

    for load in loads[:3]:
        load.wait()

    @pl.loop(0, cap)
    def _(slot):
        root[slot] = reordered_root(root[slot], order, order_t)

    pl.semaphore_wait(barrier, len(peers))

    sides = {}
    for step in range(2):
        h = core if step == 0 else 1 - core
        for side, (peer, src, dst) in enumerate(
            ((east, pl.ds(margin, margin), pl.ds(0, margin)), (west, pl.ds(0, margin), pl.ds(far, margin)))
        ):
            copy = remote(
                tile.at[:, pl.ds(h * edge, edge), :, src],
                ext.at[:, pl.ds((h + 1) * edge, edge), :, dst],
                side_send.at[step, side],
                side_recv.at[step, side],
                ty,
                peer,
            )
            when(has_east if side == 0 else has_west, copy.start)
            sides[step, side] = copy
    to_up = remote(
        tile.at[:, pl.ds(0, edge)], ext.at[:, pl.ds(3 * edge, edge), :, middle],
        rows_send.at[0, 0], rows_recv.at[0, 0], up, tx,
    )
    to_down = remote(
        tile.at[:, pl.ds(edge, edge)], ext.at[:, pl.ds(0, edge), :, middle],
        rows_send.at[1, 0], rows_recv.at[1, 0], down, tx,
    )
    when(has_up, to_up.start)
    when(has_down, to_down.start)

    has_side, has_row = (has_west, has_east), (has_up, has_down)
    across = (lax.rem(ty, n // 2) == 0, lax.rem(ty, n // 2) == n // 2 - 1)
    strips = (pl.ds(0, margin), pl.ds(far, margin))

    def straight(direction, side):
        src, dst, row = (0, 3 * edge, up) if direction == 0 else (edge, 0, down)
        return remote(
            tile.at[:, pl.ds(src, edge), :, pl.ds(margin if side == 0 else 0, margin)],
            ext.at[:, pl.ds(dst, edge), :, strips[side]],
            rows_send.at[direction, 1 + side],
            rows_recv.at[direction, 1 + side],
            row,
            east if side == 0 else west,
        )

    for direction in range(2):
        for side in range(2):
            when(across[direction] & has_row[direction] & has_side[1 - side], straight(direction, side).start)

    def corner(direction, side):
        src, dst, peer = (edge, 3 * edge, up) if direction == 0 else (2 * edge, 0, down)
        return remote(
            ext.at[:, pl.ds(src, edge), :, strips[side]],
            ext.at[:, pl.ds(dst, edge), :, strips[side]],
            rows_send.at[direction, 1 + side],
            rows_recv.at[direction, 1 + side],
            peer,
            tx,
        )

    for step in range(2):
        for side in range(2):
            when(has_side[side], sides[step, side].wait_recv)
            for direction in range(2):
                turn_now = core == (direction if step == 0 else 1 - direction)
                near = jnp.logical_not(across[direction])
                when(turn_now & near & has_side[side] & has_row[direction], corner(direction, side).start)

    for load in loads[3:]:
        load.wait()
    for (_, side), copy in sides.items():
        when(has_side[1 - side], copy.wait_send)
    for direction, copy in ((0, to_up), (1, to_down)):
        when(has_row[direction], copy.wait_send)
        when(has_row[1 - direction], copy.wait_recv)
        for side in range(2):
            near = jnp.logical_not(across[direction])
            when(near & has_row[direction] & has_side[side], corner(direction, side).wait_send)
            when(across[direction] & has_row[direction] & has_side[1 - side], straight(direction, side).wait_send)
            when(has_row[1 - direction] & has_side[side], corner(direction, side).wait_recv)

    half = margin
    tall = cells // 8 + 1
    listed = counts[ty, tx]

    def spot(slot):
        row, col = spots[0, 0, 0, slot], spots[0, 0, 1, slot]
        return lax.div(row, 8), lax.rem(row, 8), col

    @pl.loop(0, cap)
    def _(slot):
        group, skip, col = spot(slot)
        used = jnp.broadcast_to(listed, (margin, cells)) > slot

        def window(p):
            strip = ext[p, pl.ds(group, tall)]
            return cols_in(rows_in(strip, skip).reshape(cells, size), col, half)

        patch[slot, 0], patch[slot, 1] = window(0), window(1)
        to_far(
            patch[slot, 0], patch[slot, 1], probe, root[slot], used, forward, backward,
            far_v.at[slot], factor.at[slot],
        )

    chunks = probe.shape[1]
    count = part.shape[0] // chunks
    share = count // 2
    piece = share // plane_size
    mine = [c * count + core * share for c in range(chunks)]
    swaps, plane_copies = [], []
    for c in range(chunks):
        swaps.append(
            remote(
                part.at[rows_at(c * count + (1 - core) * share, share)],
                core_in.at[c],
                core_send.at[c],
                core_recv.at[c],
                mate,
                tx,
            )
        )
        copies = []
        for d in range(1, plane_size):
            other, py, px = plane_peer(d)
            copies.append(
                remote(
                    core_in.at[c, rows_at(other * piece, piece)],
                    plane_in.at[c, d],
                    plane_send.at[c, d],
                    plane_recv.at[c, d],
                    py,
                    px,
                )
            )
        plane_copies.append(copies)

    def to_plane(c):
        swaps[c].wait()
        core_in[c] = core_in[c] + part[rows_at(mine[c], share), :]
        for copy in plane_copies[c]:
            copy.start()

    for mode in range(chunks):

        @pl.loop(0, cap)
        def _(slot, mode=mode):
            if mode > 0:
                when(slot == cap - 1, lambda: to_plane(mode - 1))
            br, bi = from_far(far_v.at[slot, mode], factor.at[slot], forward, backward)
            xr, xi = patch[slot, 0], patch[slot, 1]
            pr, pi = probe[0, mode], probe[1, mode]
            for p, value in ((0, xr * br + xi * bi), (1, xr * bi - xi * br)):
                part[pl.ds((mode * 2 + p) * cells, cells), :] += value
            for p, value in ((0, pr * br + pi * bi), (1, pr * bi - pi * br)):
                if mode > 0:
                    value = value + pieces_v[slot, p]
                pieces_v[slot, p] = value

        swaps[mode].start()

    @pl.loop(0, cap)
    def _(slot):
        _, skip, col = spot(slot)
        for p in range(2):
            piece = cols_out(pieces_v[slot, p], col, half).reshape(cells // 8, 8, size)
            placed[slot, p, pl.ds(cells // 8, tall)] = rows_out(piece, skip)

    where = [spot(slot) for slot in range(cap)]

    def assemble(first, height):
        for p in range(2):
            value = 0.0
            for slot, (group, _, _) in enumerate(where):
                value = value + placed[slot, p, pl.ds((cells + first) // 8 - group, height // 8)]
            grid[p, pl.ds(first, height), :] = value.reshape(height, size)

    assemble(0, margin)
    assemble(far, margin)
    to_plane(chunks - 1)

    row_copies, across_copies = {}, {}
    cols = (strips[0], strips[1], middle)
    for i, at in enumerate(cols):
        for direction, (src, dst, peer) in enumerate(
            ((pl.ds(0, margin), from_below, up), (pl.ds(far, margin), from_above, down))
        ):
            copy = remote(
                grid.at[:, src, at], dst.at[:, :, at], down_send.at[direction, i], down_recv.at[direction, i], peer, tx
            )
            row_copies[direction, i] = copy
            if i < 2:
                over = remote(
                    grid.at[:, src, at],
                    dst.at[:, :, at],
                    down_send.at[direction, i],
                    down_recv.at[direction, i],
                    peer,
                    east if i else west,
                )
                across_copies[direction, i] = over
                when(jnp.logical_not(across[direction]) & has_row[direction], copy.start)
                when(across[direction] & has_row[direction] & has_side[i], over.start)

    assemble(margin, cells)

    line_copies = []

    def to_line(c):
        for copy in plane_copies[c]:
            copy.wait()
        own = core_in[c, rows_at(me * piece, piece), :]
        for d in range(1, plane_size):
            own = own + plane_in[c, d]
        line_in[c, line] = own
        copies = []
        for d in range(1, line_size):
            copy = remote(
                line_in.at[c, line], line_in.at[c, line], line_send.at[c, d], line_recv.at[c, d], ty, line_peer(d)
            )
            copy.start()
            copies.append(copy)
        line_copies.append(copies)

    side_copies = []

    def to_sides(step):
        for lower in (True, False):

            @pl.when(core == (0 if lower == (step == 0) else 1))
            def _(lower=lower):
                received = from_below if lower else from_above
                inner_row = (has_down if lower else has_up) & jnp.logical_not(across[1 if lower else 0])
                for side in range(2):
                    at, half_row = cols[side], 1 if lower else 0
                    side_out[side, half_row] = grid[:, pl.ds(cells if lower else margin, margin), at]

                    @pl.when(inner_row)
                    def _(side=side, at=at, half_row=half_row):
                        row_copies[1 - half_row, side].wait_recv()
                        side_out[side, half_row] = side_out[side, half_row] + received[:, :, at]

        h = 1 - core if step == 0 else core
        for side, peer in ((0, west), (1, east)):
            copy = remote(
                side_out.at[side, h], from_side.at[side, h], out_send.at[side, step], out_recv.at[side, step], ty, peer
            )
            when(has_side[side], copy.start)
            side_copies.append((side, copy))

    to_sides(0)
    to_line(0)
    to_line(1)
    for direction in range(2):
        when(has_row[direction], row_copies[direction, 2].start)
    to_sides(1)

    backs, pairs = [], []
    for c in range(chunks):
        for copy in line_copies[c]:
            copy.wait()
        done = line_in[c, 0]
        for d in range(1, line_size):
            done = done + line_in[c, d]
        place = rows_at(mine[c] + me * piece, piece)
        total[place, :] = done * (1.0 / (n * m))
        copies = []
        for d in range(1, plane_size):
            _, py, px = plane_peer(d)
            copy = remote(total.at[place], total.at[place], back_send.at[c, d], back_recv.at[c, d], py, px)
            copy.start()
            copies.append(copy)
        backs.append(copies)
        copy = remote(total.at[place], total.at[place], pair_send.at[c, 0], pair_recv.at[c, 0], mate, tx)
        copy.start()
        pairs.append(copy)

    for direction in range(2):
        when(has_row[1 - direction], row_copies[direction, 2].wait_recv)
        for i in range(2):
            there = across[1 - direction] & has_row[1 - direction] & has_side[1 - i]
            when(there, across_copies[direction, i].wait_recv)
    for side, copy in side_copies:
        when(has_side[side], copy.wait_send)
        when(has_side[1 - side], copy.wait_recv)
    for h in range(2):
        received = from_above if h == 0 else from_below
        outer = jnp.logical_not(has_up if h == 0 else has_down)
        value = grid[:, pl.ds((h + 1) * margin, margin), middle] + jnp.where(outer, 0.0, received[:, :, middle])
        from_west = jnp.where(has_west, from_side[1, h], 0.0)
        from_east = jnp.where(has_east, from_side[0, h], 0.0)
        over = across[h] & has_row[h]
        from_west = from_west + jnp.where(over & has_west, received[:, :, strips[1]], 0.0)
        from_east = from_east + jnp.where(over & has_east, received[:, :, strips[0]], 0.0)
        inner[:, pl.ds(h * margin, margin), :] = value + jnp.concatenate([from_west, from_east], 2)
    for (direction, i), copy in row_copies.items():
        if i == 2:
            when(has_row[direction], copy.wait_send)
        else:
            when(jnp.logical_not(across[direction]) & has_row[direction], copy.wait_send)
            when(across[direction] & has_row[direction] & has_side[i], across_copies[direction, i].wait_send)

    for c in range(chunks):
        for d in range(1, plane_size):
            backs[c][d - 1].wait_recv()
            source = lax.rem(me + plane_size - d, plane_size)
            at = rows_at(mine[c] + source * piece, piece)
            copy = remote(total.at[at], total.at[at], pair_send.at[c, d], pair_recv.at[c, d], mate, tx)
            copy.start()
            pairs.append(copy)
    for copies in backs:
        for copy in copies:
            copy.wait_send()
    for copy in pairs:
        copy.wait()


def shards(object_field, probe_modes, intensities, offsets, counts):
    cells = object_field.shape[1]
    margin, size = cells // 2, 2 * cells
    modes = chunks = probe_modes.shape[1]
    cap = intensities.shape[2]
    rows = 2 * modes * cells
    plane, line = lax.axis_size("ty"), lax.axis_size("tx") // 2
    share = rows // chunks // 2
    piece = share // plane
    forward, backward = tables(cells)
    order = reorder_table(cells)
    dma = pltpu.SemaphoreType.DMA
    vmem = pltpu.VMEM
    anywhere = pl.BlockSpec(memory_space=pltpu.HBM)
    inner, total = pl.pallas_call(
        kernel,
        out_shape=(jax.ShapeDtypeStruct((2, cells, cells), F32), jax.ShapeDtypeStruct((rows, cells), F32)),
        in_specs=[anywhere] * 9,
        out_specs=(VMEM, VMEM),
        scratch_shapes=[
            vmem((2, size // 8 + 1, 8, size), F32),
            vmem(probe_modes.shape, F32),
            vmem((cap, cells, cells), F32),
            vmem(forward.shape, BF16),
            vmem(backward.shape, BF16),
            vmem(order.shape, BF16),
            vmem(order.shape, BF16),
            vmem((cap, 2, margin, cells), F32),
            vmem((cap, 2, 3 * cells // 8, 8, size), F32),
            vmem((rows, cells), F32),
            vmem((2, size, size), F32),
            vmem((2, margin, size), F32),
            vmem((2, margin, size), F32),
            vmem((2, 2, 2, margin, margin), F32),
            vmem((2, 2, 2, margin, margin), F32),
            vmem((chunks, share, cells), F32),
            vmem((chunks, plane, piece, cells), F32),
            vmem((chunks, line, piece, cells), F32),
            vmem((cap, 2, cells, cells), F32),
            vmem((cap, 2, cells, cells), F32),
            vmem((cap, modes, 2, cells, cells), F32),
            pltpu.SMEM((plane, 2 * line), jnp.int32),
            pltpu.SMEM((1, 1, 2, cap), jnp.int32),
            dma((9,)),
            dma((2, 2)), dma((2, 2)), dma((2, 3)), dma((2, 3)),
            dma((2, 3)), dma((2, 3)), dma((2, 2)), dma((2, 2)),
            dma((chunks,)), dma((chunks,)),
            dma((chunks, plane)), dma((chunks, plane)), dma((chunks, line)), dma((chunks, line)),
            dma((chunks, plane)), dma((chunks, plane)), dma((chunks, plane)), dma((chunks, plane)),
        ],
        compiler_params=pltpu.CompilerParams(collective_id=0, has_side_effects=True, vmem_limit_bytes=44 * 2**20),
        name="gradient",
    )(
        *[
            pltpu.with_memory_space_constraint(x, pltpu.HBM)
            for x in (
                counts,
                offsets.swapaxes(2, 3),
                object_field.reshape(2, cells // 8, 8, cells),
                probe_modes,
                intensities,
                jnp.asarray(forward),
                jnp.asarray(backward),
                jnp.asarray(order),
                jnp.asarray(order.T),
            )
        ]
    )
    return inner, total.reshape(modes, 2, cells, cells).swapaxes(0, 1)


def solution(mesh):
    placed = (
        P(None, "ty", "tx"),
        P(),
        P("ty", "tx", None, None, None),
        P("ty", "tx", None, None),
        P(),
    )
    return jax.shard_map(
        shards, mesh=mesh, in_specs=placed, out_specs=(P(None, "ty", "tx"), P()), check_vma=False
    )
```
